256 devices in a mesh: leaf: 256 (over z, x, y, core).
Axes of the slice: x: 4, y: 4, z: 8, core: 2. Of those that a mesh axis runs over, the one named last changes fastest.
Arguments:
- leaf_inverse: float32 [2048, 256, 256], P('leaf'), may hold values from -200 to 200, as said below
- node_bases: float32 [524288, 5, 128], P('leaf'), may hold values from -6 to 6
- right_sides: float32 [524288, 128], P('leaf'), may hold values from -6 to 6
Outputs:
- solution: float32 [524288, 128], P('leaf')
- log_determinant: float32 [], replicated
The draws below stay inside these ranges and needn't reach their ends.
Inputs may be any that keep to these rules, and one draw needn't show every extreme that they name: Each leaf block of leaf_inverse is symmetric positive definite.
All inputs are finite; a program needn't handle non-finite values.
Results may differ from the reference program's by a relative error of at most 0.0003.
Values sent between devices are 32-bit elements; how exact they have to be, the bound alone decides.
A program may use at most 128 MiB of HBM per device.

```python
import jax
import jax.numpy as jnp
from jax import lax

LEAF = 256
RANK = 128
NRHS = 128
LEVELS = 5
LEAVES = 2048
NROWS = 524288


def draw_leaf_inverse(key, part):
    normals = jax.random.truncated_normal(key, -4.0, 4.0, (LEAVES, LEAF, LEAF), jnp.float32)
    gram = jnp.einsum('lij,lkj->lik', normals, normals) / LEAF
    block = gram + 0.5 * jnp.eye(LEAF, dtype=jnp.float32)[None, :, :]
    return block


def draw_node_bases(key, part):
    positions = jnp.arange(NROWS, dtype=jnp.float32)
    rising = 1.0 + 2.0 * positions / NROWS
    level_rows = jnp.array([NROWS // 2 ** (LEVELS - 1 - level_index) for level_index in range(LEVELS)], jnp.float32)
    level_scale = jnp.sqrt(2.0 / level_rows)
    entries = jax.random.truncated_normal(key, -5.0, 5.0, (NROWS, LEVELS, RANK), jnp.float32)
    return entries * rising[:, None, None] * level_scale[None, :, None]


def levels(own_key, extent, shards, smallest, high):
    loudness = 1.0
    for dim, blocks in shards:
        heights = jax.random.uniform(jax.random.fold_in(jax.random.fold_in(own_key, 6), dim), (blocks,), jnp.float32, smallest / len(shards), high / len(shards))
        loudness = loudness * jnp.repeat(jnp.exp(heights), extent[dim] // blocks).reshape((-1,) + (1,) * (len(extent) - 1 - dim))
    return loudness


def gaussian(key, dims, scale, limit, cuts=(), kind=jnp.bfloat16):
    loudness = levels(key, dims, cuts, -0.22, 0.18) if cuts else 1.0
    drawn = jax.random.normal(key, dims, jnp.float32) * scale * loudness
    return jnp.minimum(jnp.maximum(drawn, -limit), limit).astype(kind)


def setup_inputs(seed: int = 0) -> dict:
    streams_of = jax.random.split(jax.random.key(seed), 4)
    return {
        "leaf_inverse": draw_leaf_inverse(jax.random.fold_in(streams_of[3], 71), 0),
        "node_bases": draw_node_bases(jax.random.fold_in(streams_of[3], 71), 0),
        "right_sides": gaussian(streams_of[2], (NROWS, NRHS), 1.0, 6.0, ((0, 256),), jnp.float32),
    }


def cholesky_solve(factor, targets):
    middle = lax.linalg.triangular_solve(factor, targets, left_side=True, lower=True)
    return lax.linalg.triangular_solve(factor, middle, left_side=True, lower=True, transpose_a=True)

def reference(leaf_inverse, node_bases, right_sides):
    row_count = right_sides.shape[0]
    columns = jnp.concatenate([node_bases.reshape(row_count, LEVELS * RANK), right_sides], axis=1)
    blocks = columns.reshape(LEAVES, LEAF, -1)
    current = jnp.einsum('lij,ljc->lic', leaf_inverse, blocks, precision=lax.Precision.HIGHEST)
    current = current.reshape(row_count, -1)
    total_log = jnp.zeros((), jnp.float32)
    for level_index in range(LEVELS):
        node_count = 2 ** (LEVELS - 1 - level_index)
        basis = node_bases[:, level_index, :].reshape(node_count, -1, RANK)
        stacked = current.reshape(node_count, row_count // node_count, -1)
        products = jnp.einsum('nir,nic->nrc', basis, stacked, precision=lax.Precision.HIGHEST)
        capacity = jnp.eye(RANK, dtype=jnp.float32)[None, :, :] + products[:, :, :RANK]
        factor = jnp.linalg.cholesky(capacity)
        weights = cholesky_solve(factor, products[:, :, RANK:])
        update = jnp.einsum('nir,nrc->nic', stacked[:, :, :RANK], weights, precision=lax.Precision.HIGHEST)
        current = (stacked[:, :, RANK:] - update).reshape(row_count, -1)
        total_log = total_log + 2.0 * jnp.sum(jnp.log(jnp.diagonal(factor, axis1=1, axis2=2)))
    return (current, total_log / (RANK * (2 ** LEVELS - 1)))
```

```python
import functools

import jax
import jax.numpy as jnp
from jax import lax
from jax.experimental import pallas as pl
from jax.experimental.pallas import tpu as pltpu
from jax.sharding import PartitionSpec as P

F32 = jnp.float32
BF16 = jnp.bfloat16
MESH = pl.DeviceIdType.MESH
R = 128
LEVELS = 5
OFFSET = (0, 6, 11, 15, 18, 20)
GROUP = 16
STEP = 16


def block(a, b):
    return OFFSET[a] + b - a


def halves(v):
    high = v.astype(BF16)
    return high, (v - high.astype(F32)).astype(BF16)


def dot3(a, b):
    ah, al = halves(a)
    bh, bl = halves(b)
    return jnp.dot(
        jnp.concatenate([ah, ah, al], axis=1),
        jnp.concatenate([bh, bl, bh], axis=0),
        preferred_element_type=F32,
    )


def tdot(a, b):
    return lax.dot_general(a, b, (((0,), (0,)), ((), ())), preferred_element_type=F32)


def tdot3(a, b):
    ah, al = halves(a)
    bh, bl = halves(b)
    return tdot(jnp.concatenate([ah, ah, al], axis=0), jnp.concatenate([bh, bl, bh], axis=0))


def dot_full(a, b):
    return jnp.dot(a, b, precision=lax.Precision.HIGHEST, preferred_element_type=F32)


def thirds(v):
    high = v.astype(BF16)
    rest = v - high.astype(F32)
    middle = rest.astype(BF16)
    low = (rest - middle.astype(F32)).astype(BF16)
    return high, middle, low


def sweep(a_ref):
    lane = lax.broadcasted_iota(jnp.int32, (STEP, R), 1)
    sub = lax.broadcasted_iota(jnp.int32, (STEP, R), 0)
    sub8 = lax.broadcasted_iota(jnp.int32, (8, R), 0)
    row_step = lax.broadcasted_iota(jnp.int32, (R, R), 0) // STEP
    column_step = lax.broadcasted_iota(jnp.int32, (R, R), 1) // STEP

    def pack(rows):
        groups = []
        for first in range(0, STEP, 8):
            packed = rows[first]
            for i in range(1, 8):
                packed = jnp.where(sub8 == i, rows[first + i], packed)
            groups.append(packed)
        return jnp.concatenate(groups, axis=0)

    def step(p, logs):
        base = pl.multiple_of(p * STEP, STEP)
        panel = a_ref[pl.ds(base, STEP), :]
        turned = pltpu.roll(panel, lax.rem(R - base, R), axis=1)
        q = jnp.where(lane // STEP == p, jnp.where(lane - base == sub, -1.0, 0.0), panel)
        rows = []
        for i in range(STEP):
            entries = [jnp.broadcast_to(turned[i : i + 1, j : j + 1], (8, R)) for j in range(i, STEP)]
            entries.append(jnp.broadcast_to(q[i : i + 1, :], (8, R)))
            rows.append(jnp.stack(entries))
        inverses = []
        for k in range(STEP):
            inverses.append(1.0 / rows[k][0])
            for i in range(k + 1, STEP):
                ratio = rows[k][i - k] * inverses[k]
                rows[i] = rows[i] - ratio[None] * rows[k][i - k :]
        v = pack([rows[i][STEP - i] for i in range(STEP)])
        w = v * pack(inverses)
        pivots = pack([rows[i][0] for i in range(STEP)])
        vh, vm, vl = thirds(v)
        wh, wm, wl = thirds(w)
        change = tdot(
            jnp.concatenate([vh, vh, vm, vh, vm, vl], axis=0),
            jnp.concatenate([wh, wm, wh, wl, wm, wh], axis=0),
        )
        a_ref[...] = jnp.where((row_step == p) | (column_step == p), 0.0, a_ref[...]) - change
        taken = jnp.log(pivots)
        return logs + taken[:8] + taken[8:]

    return lax.fori_loop(0, R // STEP, step, jnp.zeros((8, R), F32))


def kernel(
    d_hbm, u_hbm, b_hbm, o_hbm, log_ref,
    dv, uv, bv, xv, ov, g, r0, rc, h, r1,
    pc0, pc1, pc2, pc3, pc4, sx1, sx2, sx3, sx4, rx1, rx2, rx3, rx4,
    f0, f1, f2, f3, f4, t0, t1, t2, t3, gt, a_ref, y,
    load_sem, out_sem, rs_send, rs_recv, x_send, x_recv, ag_send, ag_recv,
):
    leaves = d_hbm.shape[0]
    size = d_hbm.shape[1]
    pc = (pc0, pc1, pc2, pc3, pc4)
    sx = (None, sx1, sx2, sx3, sx4)
    rx = (None, rx1, rx2, rx3, rx4)
    f = (f0, f1, f2, f3, f4)
    t = (t0, t1, t2, t3)

    me = lax.axis_index("leaf")
    z = me // 32
    x = (me // 8) % 4
    half = x // 2
    x_in = x + half * (3 - 2 * x)
    seat = x_in * 8 + me % 8
    chip = seat // 2
    core = seat % 2
    piece = pl.multiple_of(seat * 8, 8)

    def device(other):
        xo = other // 8
        return z * 32 + (xo + half * (3 - 2 * xo)) * 8 + other % 8

    partner = (
        None,
        me + 8 * (3 - 2 * x),
        me + 32 * (1 - 2 * (z % 2)),
        me + 32 * (3 - 2 * (z % 4)),
        me + 32 * (7 - 2 * z),
    )

    barrier = pltpu.get_barrier_semaphore()

    def greet(r, carry):
        pl.semaphore_signal(barrier, inc=1, device_id=(device((seat + r) % GROUP),), device_id_type=MESH)
        return carry

    lax.fori_loop(1, GROUP, greet, 0)
    for e in range(1, LEVELS):
        pl.semaphore_signal(barrier, inc=1, device_id=(partner[e],), device_id_type=MESH)

    def rows_of(leaf):
        return pl.ds(pl.multiple_of(leaf * size, size), size)

    def load_d(leaf):
        return pltpu.make_async_copy(d_hbm.at[leaf], dv.at[leaf], load_sem.at[0, leaf])

    def load_u0(leaf):
        return pltpu.make_async_copy(
            u_hbm.at[pl.ds(0, 1), rows_of(leaf), :], uv.at[pl.ds(0, 1), rows_of(leaf), :], load_sem.at[1, leaf]
        )

    def load_u(leaf):
        return pltpu.make_async_copy(
            u_hbm.at[pl.ds(1, LEVELS - 1), rows_of(leaf), :],
            uv.at[pl.ds(1, LEVELS - 1), rows_of(leaf), :],
            load_sem.at[2, leaf],
        )

    def load_b(leaf):
        return pltpu.make_async_copy(b_hbm.at[rows_of(leaf), :], bv.at[rows_of(leaf), :], load_sem.at[3, leaf])

    for leaf in range(leaves):
        load_d(leaf).start()
        load_u0(leaf).start()
    for leaf in range(leaves):
        load_u(leaf).start()
        load_b(leaf).start()

    def remote(source, target, send, recv, who):
        return pltpu.make_async_remote_copy(
            src_ref=source, dst_ref=target, send_sem=send, recv_sem=recv,
            device_id=(who,), device_id_type=MESH,
        )

    def first_leaf(leaf, total):
        load_d(leaf).wait()
        load_u0(leaf).wait()
        u0 = uv[0, rows_of(leaf), :]
        x0 = dot3(dv[leaf], u0)
        xv[0, rows_of(leaf), :] = x0
        return total + tdot3(u0, x0)

    total = lax.fori_loop(0, leaves, first_leaf, jnp.zeros((R, R), F32))
    g[0] = total.reshape(8, 2, 8, R)

    pl.semaphore_wait(barrier, GROUP - 1 + LEVELS - 1)

    def send_first(r, carry):
        other = (seat + r) % GROUP
        remote(
            g.at[pl.ds(0, 1), other // 2, other % 2], r0.at[r - 1],
            rs_send.at[0], rs_recv.at[0], device(other),
        ).start()
        return carry

    lax.fori_loop(1, GROUP, send_first, 0)

    g[pl.ds(1, 19)] = jnp.zeros((19, 8, 2, 8, R), F32)

    def add_block(a, b, value):
        g[block(a, b)] = g[block(a, b)] + value.reshape(8, 2, 8, R)

    def next_leaf(leaf, carry):
        load_u(leaf).wait()
        load_b(leaf).wait()
        u = [uv[j, rows_of(leaf), :] for j in range(LEVELS)]
        values = jnp.concatenate(u[1:] + [bv[rows_of(leaf), :]], axis=1)
        got = dot3(dv[leaf], values)
        for k in range(1, LEVELS + 1):
            xv[k, rows_of(leaf), :] = got[:, R * (k - 1) : R * k]
        for columns, top in (((1, 2), 2), ((3, 4), 4), ((5,), 4)):
            part = got[:, R * (columns[0] - 1) : R * columns[-1]]
            products = tdot3(jnp.concatenate(u[: top + 1], axis=1), part)
            for k in columns:
                for j in range(min(k, LEVELS - 1) + 1):
                    at = R * (k - columns[0])
                    add_block(j, k, products[R * j : R * (j + 1), at : at + R])
        return carry

    def sum_first():
        remote(r0, r0, rs_send.at[0], rs_recv.at[0], me).wait_recv()
        kept = g[0, chip, core]
        for r in range(GROUP - 1):
            kept = kept + r0[r, 0]
        pc0[0] = kept

    def gather(level, first, count, slot):
        for b in range(first, first + count):
            f[level][b, pl.ds(piece, 8), :] = pc[level][b]

        def one(r, carry):
            other = (seat + r) % GROUP
            remote(
                pc[level].at[pl.ds(first, count)],
                f[level].at[pl.ds(first, count), pl.ds(piece, 8), :],
                ag_send.at[level, slot], ag_recv.at[level, slot], device(other),
            ).start()
            return carry

        lax.fori_loop(1, GROUP, one, 0)

    def gathered(level, first, count, slot):
        ref = f[level].at[pl.ds(first, count), pl.ds(0, 120), :]
        return remote(ref, ref, ag_send.at[level, slot], ag_recv.at[level, slot], me)

    lax.fori_loop(0, leaves // 2, next_leaf, 0)
    sum_first()
    gather(0, 0, 1, 0)
    lax.fori_loop(leaves // 2, leaves, next_leaf, 0)

    mate = me + 1 - 2 * core
    to_mate = remote(
        g.at[pl.ds(1, 19), pl.ds(0, 8), 1 - core], rc, rs_send.at[1], rs_recv.at[1], mate
    )
    to_mate.start()
    to_mate.wait_recv()

    def add_core(i, carry):
        h[i] = g[i + 1, :, core] + rc[i]
        return carry

    lax.fori_loop(0, 19, add_core, 0)

    def send_rest(r, carry):
        other = (chip + r) % 8
        remote(
            h.at[pl.ds(0, 19), other], r1.at[r - 1],
            rs_send.at[2], rs_recv.at[2], device(other * 2 + core),
        ).start()
        return carry

    lax.fori_loop(1, 8, send_rest, 0)

    eye = (
        lax.broadcasted_iota(jnp.int32, (R, R), 0) == lax.broadcasted_iota(jnp.int32, (R, R), 1)
    ).astype(F32)
    logs = jnp.zeros((8, R), F32)

    for level in range(LEVELS):
        gathered(level, 0, 1, 0).wait_recv()
        a_ref[...] = f[level][0] + eye
        logs = logs + sweep(a_ref)
        inverse = -a_ref[...]
        count = LEVELS - level
        if level == 0:
            remote(r1, r1, rs_send.at[2], rs_recv.at[2], me).wait_recv()
            kept = h[:, chip]
            for r in range(7):
                kept = kept + r1[r]
            pc0[pl.ds(1, 19)] = kept
            gather(0, 1, count, 1)
        gathered(level, 1, count, 1).wait_recv()
        if level == LEVELS - 1:
            y[pl.ds(R * level, R), :] = dot_full(inverse, f[level][1])
            break
        row = jnp.concatenate([f[level][i] for i in range(1, count + 1)], axis=1)
        ratio = dot_full(inverse, row)
        t[level][...] = ratio
        for a in range(count - 1):
            gt[a] = f[level][a + 1].T
        left = jnp.concatenate([gt[a, pl.ds(piece, 8), :] for a in range(count - 1)], axis=0)
        down = dot_full(left, ratio)
        e = level + 1
        skip = OFFSET[e] - OFFSET[level]
        for a in range(e, LEVELS):
            for b in range(a, LEVELS + 1):
                i = block(a, b) - OFFSET[e]
                sx[e][i] = pc[level][i + skip] - down[8 * (a - e) : 8 * (a - e) + 8, R * (b - e) : R * (b - e) + R]
        total_blocks = 20 - OFFSET[e]
        sx[e][total_blocks] = logs
        swap = [
            remote(
                sx[e].at[pl.ds(first, n)], rx[e].at[pl.ds(first, n)],
                x_send.at[e, slot], x_recv.at[e, slot], partner[e],
            )
            for slot, first, n in ((0, 0, 1), (1, 1, total_blocks))
        ]
        swap[0].start()
        swap[1].start()
        swap[0].wait_recv()
        pc[e][0] = sx[e][0] + rx[e][0]
        gather(e, 0, 1, 0)
        swap[1].wait_recv()
        pc[e][pl.ds(1, total_blocks)] = sx[e][pl.ds(1, total_blocks)] + rx[e][pl.ds(1, total_blocks)]
        gather(e, 1, count - 1, 1)
        logs = pc[e][total_blocks]

    for level in range(LEVELS - 2, -1, -1):
        known = R * (LEVELS - 1 - level)
        y[pl.ds(R * level, R), :] = t[level][:, known:] - dot_full(
            t[level][:, :known], y[pl.ds(R * (level + 1), known), :]
        )
    y_high, y_low = halves(y[...])
    y_stack = jnp.concatenate([y_high, y_low, y_high], axis=0)

    def store(leaf):
        return pltpu.make_async_copy(ov.at[rows_of(leaf), :], o_hbm.at[rows_of(leaf), :], out_sem.at[leaf])

    def last_leaf(leaf, carry):
        have = jnp.concatenate([xv[k, rows_of(leaf), :] for k in range(LEVELS)], axis=1)
        high, low = halves(have)
        change = jnp.dot(jnp.concatenate([high, high, low], axis=1), y_stack, preferred_element_type=F32)
        ov[rows_of(leaf), :] = xv[LEVELS, rows_of(leaf), :] - change
        store(leaf).start()
        return carry

    lax.fori_loop(0, leaves, last_leaf, 0)
    log_ref[0, 0] = jnp.sum(logs) / (R * R * (2**LEVELS - 1))

    remote(r0, r0, rs_send.at[0], rs_recv.at[0], me).wait_send()
    to_mate.wait_send()
    remote(r1, r1, rs_send.at[2], rs_recv.at[2], me).wait_send()
    for level in range(LEVELS):
        gathered(level, 0, 1, 0).wait_send()
        gathered(level, 1, LEVELS - level, 1).wait_send()
    for e in range(1, LEVELS):
        n = 20 - OFFSET[e]
        remote(sx[e].at[pl.ds(0, 1)], rx[e].at[pl.ds(0, 1)], x_send.at[e, 0], x_recv.at[e, 0], me).wait_send()
        remote(sx[e].at[pl.ds(1, n)], rx[e].at[pl.ds(1, n)], x_send.at[e, 1], x_recv.at[e, 1], me).wait_send()

    def finish(leaf, carry):
        store(leaf).wait()
        return carry

    lax.fori_loop(0, leaves, finish, 0)


def body(leaf_inverse, node_bases, right_sides):
    leaves, size = leaf_inverse.shape[:2]
    rows = right_sides.shape[0]
    bases = jnp.transpose(node_bases, (1, 0, 2))
    vm = pltpu.VMEM
    sizes = [20 - OFFSET[e] + 1 for e in range(LEVELS)]
    any_spec = pl.BlockSpec(memory_space=pl.ANY)
    scratch = [
        vm((leaves, size, size), F32), vm((LEVELS, rows, R), F32), vm((rows, R), F32),
        vm((LEVELS + 1, rows, R), F32), vm((rows, R), F32),
        vm((20, 8, 2, 8, R), F32), vm((GROUP - 1, 1, 8, R), F32), vm((19, 8, 8, R), F32),
        vm((19, 8, 8, R), F32), vm((7, 19, 8, R), F32),
    ]
    scratch += [vm((n, 8, R), F32) for n in [20] + sizes[1:]]
    scratch += [vm((n, 8, R), F32) for n in sizes[1:]]
    scratch += [vm((n, 8, R), F32) for n in sizes[1:]]
    scratch += [vm((LEVELS + 1 - level, R, R), F32) for level in range(LEVELS)]
    scratch += [vm((R, R * (LEVELS - level)), F32) for level in range(LEVELS - 1)]
    scratch += [vm((LEVELS - 1, R, R), F32), vm((R, R), F32), vm((LEVELS * R, R), F32)]
    dma = pltpu.SemaphoreType.DMA
    scratch += [
        dma((4, leaves)), dma((leaves,)), dma((3,)), dma((3,)),
        dma((LEVELS, 2)), dma((LEVELS, 2)), dma((LEVELS, 2)), dma((LEVELS, 2)),
    ]
    solution, log_total = pl.pallas_call(
        kernel,
        out_shape=(
            jax.ShapeDtypeStruct((rows, R), F32),
            jax.ShapeDtypeStruct((1, 1), F32),
        ),
        in_specs=[any_spec] * 3,
        out_specs=(any_spec, pl.BlockSpec(memory_space=pltpu.SMEM)),
        scratch_shapes=scratch,
        compiler_params=pltpu.CompilerParams(
            collective_id=0, has_side_effects=True, vmem_limit_bytes=60 * 2**20
        ),
    )(leaf_inverse, bases, right_sides)
    return solution, log_total.reshape(())


def solution(mesh):
    return jax.shard_map(
        body,
        mesh=mesh,
        in_specs=(P("leaf", None, None), P("leaf", None, None), P("leaf", None)),
        out_specs=(P("leaf", None), P()),
        check_vma=False,
    )
```

```python
import functools

import jax
import jax.numpy as jnp
from jax import lax
from jax.experimental import pallas as pl
from jax.experimental.pallas import tpu as pltpu
from jax.sharding import PartitionSpec as P

F32 = jnp.float32
BF16 = jnp.bfloat16
MESH = pl.DeviceIdType.MESH
R = 128
LEVELS = 5
LEVEL_COLUMNS = LEVELS + 1
GROUP = 16
STEP = 16

ORDER = (
    (0, 0), (0, 1), (1, 1),
    (0, 2), (0, 3), (1, 2), (2, 2), (1, 3), (2, 3), (3, 3),
    (0, 4), (0, 5), (1, 4), (1, 5), (2, 4), (2, 5), (3, 4), (4, 4), (3, 5), (4, 5),
)
COUNT = len(ORDER)
A, B, END = 3, 10, COUNT
GATHERS = {
    "d0": (0, 1), "c0": (1, 3), "a0": (3, 5), "b0": (10, 12), "a1": (5, 8), "b1": (12, 14),
    "a2": (8, 10), "b2": (14, 16), "b3": (16, 19), "b4": (19, 20),
}
SWAPS = {"a1": (5, 10), "b1": (12, 20), "a2": (8, 10), "b2": (14, 20), "b3": (16, 20), "b4": (19, 20)}
GATHER_SLOT = {name: i for i, name in enumerate(GATHERS)}
SWAP_SLOT = {name: i for i, name in enumerate(SWAPS)}


def block(a, b):
    return ORDER.index((a, b))


def halves(v):
    high = v.astype(BF16)
    return high, (v - high.astype(F32)).astype(BF16)


def dot3(a, b):
    ah, al = halves(a)
    bh, bl = halves(b)
    return jnp.dot(
        jnp.concatenate([ah, ah, al], axis=1),
        jnp.concatenate([bh, bl, bh], axis=0),
        preferred_element_type=F32,
    )


def tdot(a, b):
    return lax.dot_general(a, b, (((0,), (0,)), ((), ())), preferred_element_type=F32)


def tdot3(a, b):
    ah, al = halves(a)
    bh, bl = halves(b)
    return tdot(jnp.concatenate([ah, ah, al], axis=0), jnp.concatenate([bh, bl, bh], axis=0))


def dot_full(a, b):
    return jnp.dot(a, b, precision=lax.Precision.HIGHEST, preferred_element_type=F32)


def thirds(v):
    high = v.astype(BF16)
    rest = v - high.astype(F32)
    middle = rest.astype(BF16)
    low = (rest - middle.astype(F32)).astype(BF16)
    return high, middle, low


def sweep(a_ref, column_ref, q_ref, log_ref, tasks):
    lane = lax.broadcasted_iota(jnp.int32, (STEP, R), 1)
    sub = lax.broadcasted_iota(jnp.int32, (STEP, R), 0)
    sub8 = lax.broadcasted_iota(jnp.int32, (8, R), 0)
    row_step = lax.broadcasted_iota(jnp.int32, (R, R), 0) // STEP
    column_step = lax.broadcasted_iota(jnp.int32, (R, R), 1) // STEP

    def pack(rows):
        groups = []
        for first in range(0, STEP, 8):
            packed = rows[first]
            for i in range(1, 8):
                packed = jnp.where(sub8 == i, rows[first + i], packed)
            groups.append(packed)
        return jnp.concatenate(groups, axis=0)

    def step(p, carry):
        for at, task in tasks.items():
            pl.when(p == at)(task)
        base = pl.multiple_of(p * STEP, STEP)
        panel = a_ref[pl.ds(base, STEP), :]
        turned = pltpu.roll(panel, lax.rem(R - base, R), axis=1)
        for j in range(STEP):
            high = (j // 8 + 1) * 8
            column_ref[pl.ds(j * STEP, high), :] = jnp.broadcast_to(turned[:high, j : j + 1], (high, R))
        q_ref[pl.ds(0, STEP), :] = jnp.where(
            lane // STEP == p, jnp.where(lane - base == sub, -1.0, 0.0), panel
        )
        rows, ratios, inverses = [], [], []
        for i in range(STEP):
            row = [column_ref[pl.ds(j * STEP + i, 8, stride=0), :] for j in range(i, STEP)]
            row.append(q_ref[pl.ds(i, 8, stride=0), :])
            row = jnp.stack(row)
            for m in range(i):
                row = row - ratios[m][i - m][None] * rows[m][i - m :]
            inverse = 1.0 / row[0]
            rows.append(row)
            inverses.append(inverse)
            ratios.append(row[: STEP - i] * inverse[None])
        v = pack([rows[i][STEP - i] for i in range(STEP)])
        w = v * pack(inverses)
        pivots = pack([rows[i][0] for i in range(STEP)])
        vh, vm, vl = thirds(v)
        wh, wm, wl = thirds(w)
        change = tdot(
            jnp.concatenate([vh, vh, vm, vh, vm, vl], axis=0),
            jnp.concatenate([wh, wm, wh, wl, wm, wh], axis=0),
        )
        a_ref[...] = jnp.where((row_step == p) | (column_step == p), 0.0, a_ref[...]) - change
        taken = jnp.log(pivots)
        log_ref[...] = log_ref[...] + taken[:8] + taken[8:]
        return carry

    lax.fori_loop(0, R // STEP, step, 0)


def kernel(
    d_hbm, u_hbm, b_hbm, o_hbm, total_ref,
    dv, uv, bv, xv, ov, ab, g, rd, rs, ra, rb, ha, hb, qa, qb,
    pc, sx, rx, dx, dr, f, iv, tv, gt, zv, a_ref, column_ref, q_ref, log_ref,
    load_sem, out_sem, rs_send, rs_recv, d_send, d_recv, x_send, x_recv, g_send, g_recv,
):
    leaves = d_hbm.shape[0]
    size = d_hbm.shape[1]

    me = lax.axis_index("leaf")
    z = me // 32
    x = (me // 8) % 4
    half = x // 2
    x_in = x + half * (3 - 2 * x)
    seat = x_in * 8 + me % 8
    chip = seat // 2
    core = seat % 2
    piece = pl.multiple_of(seat * 8, 8)

    def device(other):
        xo = other // 8
        return z * 32 + (xo + half * (3 - 2 * xo)) * 8 + other % 8

    mate = me + 1 - 2 * core
    partner = (
        None,
        me + 8 * (3 - 2 * x),
        me + 32 * (1 - 2 * (z % 2)),
        me + 32 * (3 - 2 * (z % 4)),
        me + 32 * (7 - 2 * z),
    )

    barrier = pltpu.get_barrier_semaphore()

    def greet(r, carry):
        pl.semaphore_signal(barrier, inc=1, device_id=(device((seat + r) % GROUP),), device_id_type=MESH)
        return carry

    lax.fori_loop(1, GROUP, greet, 0)
    for e in range(1, LEVELS):
        pl.semaphore_signal(barrier, inc=1, device_id=(partner[e],), device_id_type=MESH)

    def rows_of(leaf):
        return pl.ds(pl.multiple_of(leaf * size, size), size)

    def load_d(leaf):
        return pltpu.make_async_copy(d_hbm.at[leaf], dv.at[leaf], load_sem.at[0, leaf])

    def load_u(leaf, first, count, slot):
        at = (pl.ds(first, count), rows_of(leaf), slice(None))
        return pltpu.make_async_copy(u_hbm.at[at], uv.at[at], load_sem.at[slot, leaf])

    def load_b(leaf):
        return pltpu.make_async_copy(b_hbm.at[rows_of(leaf), :], bv.at[rows_of(leaf), :], load_sem.at[4, leaf])

    for leaf in range(leaves):
        load_d(leaf).start()
        load_u(leaf, 0, 2, 1).start()
    for leaf in range(leaves):
        load_u(leaf, 2, 2, 2).start()
    for leaf in range(leaves):
        load_u(leaf, 4, 1, 3).start()
        load_b(leaf).start()

    def remote(source, target, send, recv, who):
        return pltpu.make_async_remote_copy(
            src_ref=source, dst_ref=target, send_sem=send, recv_sem=recv,
            device_id=(who,), device_id_type=MESH,
        )

    g[...] = jnp.zeros((COUNT, 8, 2, 8, R), F32)

    def columns_of(leaf, columns):
        top = min(columns[-1], LEVELS - 1)
        u = [uv[j, rows_of(leaf), :] for j in range(top + 1)]
        have = [u[k] if k < LEVELS else bv[rows_of(leaf), :] for k in columns]
        got = dot3(dv[leaf], jnp.concatenate(have, axis=1))
        products = tdot3(jnp.concatenate(u, axis=1), got)
        for i, k in enumerate(columns):
            xv[k, rows_of(leaf), :] = got[:, R * i : R * (i + 1)]
            for j in range(min(k, LEVELS - 1) + 1):
                at = block(j, k)
                g[at] = g[at] + products[R * j : R * (j + 1), R * i : R * (i + 1)].reshape(8, 2, 8, R)

    def leaf_first(leaf, carry):
        load_d(leaf).wait()
        load_u(leaf, 0, 2, 1).wait()
        columns_of(leaf, (0, 1))
        return carry

    def leaf_second(leaf, carry):
        load_u(leaf, 2, 2, 2).wait()
        columns_of(leaf, (2, 3))
        return carry

    def leaf_third(leaf, carry):
        load_u(leaf, 4, 1, 3).wait()
        load_b(leaf).wait()
        columns_of(leaf, (4, 5))
        return carry

    def scatter(first, count, target, slot):
        def one(r, carry):
            other = (seat + r) % GROUP
            remote(
                g.at[pl.ds(first, count), other // 2, other % 2], target.at[r - 1],
                rs_send.at[slot], rs_recv.at[slot], device(other),
            ).start()
            return carry

        lax.fori_loop(1, GROUP, one, 0)

    def scattered(first, count, target, slot):
        remote(target, target, rs_send.at[slot], rs_recv.at[slot], me).wait_recv()
        kept = g[pl.ds(first, count), chip, core]
        for r in range(GROUP - 1):
            kept = kept + target[r]
        pc[pl.ds(first, count)] = kept

    def to_mate(first, count, target, slot):
        return remote(
            g.at[pl.ds(first, count), pl.ds(0, 8), 1 - core], target, rs_send.at[slot], rs_recv.at[slot], mate
        )

    def scatter_chips(first, count, from_mate, summed, target, slot):
        to_mate(first, count, from_mate, slot - 1).wait_recv()

        def add(i, carry):
            summed[i] = g[i + first, :, core] + from_mate[i]
            return carry

        lax.fori_loop(0, count, add, 0)

        def one(r, carry):
            other = (chip + r) % 8
            remote(
                summed.at[pl.ds(0, count), other], target.at[r - 1],
                rs_send.at[slot], rs_recv.at[slot], device(other * 2 + core),
            ).start()
            return carry

        lax.fori_loop(1, 8, one, 0)

    def scattered_chips(first, count, summed, target, slot):
        remote(target, target, rs_send.at[slot], rs_recv.at[slot], me).wait_recv()
        kept = summed[:, chip]
        for r in range(7):
            kept = kept + target[r]
        pc[pl.ds(first, count)] = kept

    def gather(name):
        first, last = GATHERS[name]
        slot = GATHER_SLOT[name]
        f[pl.ds(first, last - first), pl.ds(piece, 8), :] = pc[pl.ds(first, last - first)]

        def one(r, carry):
            other = (seat + r) % GROUP
            remote(
                pc.at[pl.ds(first, last - first)],
                f.at[pl.ds(first, last - first), pl.ds(piece, 8), :],
                g_send.at[slot], g_recv.at[slot], device(other),
            ).start()
            return carry

        lax.fori_loop(1, GROUP, one, 0)

    def gathered(name):
        first, last = GATHERS[name]
        slot = GATHER_SLOT[name]
        ref = f.at[pl.ds(first, last - first), pl.ds(0, 120), :]
        return remote(ref, ref, g_send.at[slot], g_recv.at[slot], me)

    def diagonal(e):
        return remote(dx.at[e - 1], dr.at[e - 1], d_send.at[e - 1], d_recv.at[e - 1], partner[e])

    def swap(name):
        first, last = SWAPS[name]
        e = int(name[1])
        slot = SWAP_SLOT[name]
        at = pl.ds(first, last - first)
        return remote(sx.at[e - 1, at], rx.at[e - 1, at], x_send.at[slot], x_recv.at[slot], partner[e])

    def turn(level, k):
        gt[level, k] = f[block(level, k)].T

    def critical(level):
        e = level + 1
        ratio = dot_full(iv[level], f[block(level, e)])
        tv[level, e] = ratio
        dx[e - 1, pl.ds(0, R), :] = f[block(e, e)] - dot_full(gt[level, e], ratio)
        dx[e - 1, pl.ds(R, 8), :] = log_ref[...]
        diagonal(e).start()

    def lower(level, columns, name):
        e = level + 1
        first, last = SWAPS[name]
        fresh = [k for k in columns if k != e]
        ratio = dot_full(iv[level], jnp.concatenate([f[block(level, k)] for k in fresh], axis=1))
        for i, k in enumerate(fresh):
            tv[level, k] = ratio[:, R * i : R * (i + 1)]
            if k < LEVELS:
                turn(level, k)
        ends = [r for r in range(e, LEVELS) if r <= columns[-1]]
        left = jnp.concatenate([gt[level, r, pl.ds(piece, 8), :] for r in ends], axis=0)
        down = dot_full(left, ratio)
        for at in range(first, last):
            r, k = ORDER[at]
            i = fresh.index(k)
            sx[e - 1, at] = pc[at] - down[8 * (r - e) : 8 * (r - e) + 8, R * i : R * (i + 1)]
        swap(name).start()

    def merge(name):
        first, last = SWAPS[name]
        e = int(name[1])
        swap(name).wait_recv()
        at = pl.ds(first, last - first)
        pc[at] = sx[e - 1, at] + rx[e - 1, at]
        gather(name)

    def enter(e):
        diagonal(e).wait_recv()
        a_ref[...] = dx[e - 1, pl.ds(0, R), :] + dr[e - 1, pl.ds(0, R), :] + eye
        log_ref[...] = dx[e - 1, pl.ds(R, 8), :] + dr[e - 1, pl.ds(R, 8), :]

    def invert(level, tasks):
        sweep(a_ref, column_ref, q_ref, log_ref, tasks)
        iv[level] = -a_ref[...]

    eye = (
        lax.broadcasted_iota(jnp.int32, (R, R), 0) == lax.broadcasted_iota(jnp.int32, (R, R), 1)
    ).astype(F32)

    lax.fori_loop(0, leaves, leaf_first, 0)
    pl.semaphore_wait(barrier, GROUP - 1 + LEVELS - 1)
    scatter(0, 1, rd, 0)
    scatter(1, 2, rs, 1)
    lax.fori_loop(0, leaves, leaf_second, 0)
    scattered(0, 1, rd, 0)
    gather("d0")
    to_mate(A, B - A, ra, 2).start()
    lax.fori_loop(0, leaves, leaf_third, 0)
    to_mate(B, END - B, rb, 4).start()
    scattered(1, 2, rs, 1)
    gather("c0")
    scatter_chips(A, B - A, ra, ha, qa, 3)
    gathered("d0").wait_recv()
    a_ref[...] = f[0] + eye
    log_ref[...] = jnp.zeros((8, R), F32)

    def task_0():
        scatter_chips(B, END - B, rb, hb, qb, 5)

    invert(0, {4: task_0})
    gathered("c0").wait_recv()
    turn(0, 1)
    critical(0)
    scattered_chips(A, B - A, ha, qa, 3)
    gather("a0")
    scattered_chips(B, END - B, hb, qb, 5)
    gather("b0")
    gathered("a0").wait_recv()
    lower(0, (2, 3), "a1")

    enter(1)

    def task_1a():
        merge("a1")

    def task_1b():
        gathered("b0").wait_recv()
        lower(0, (4, 5), "b1")

    invert(1, {3: task_1a, 5: task_1b})
    gathered("a1").wait_recv()
    turn(1, 2)
    critical(1)
    lower(1, (2, 3), "a2")
    merge("b1")

    enter(2)
    merge("a2")

    def task_2a():
        gathered("b1").wait_recv()
        lower(1, (4, 5), "b2")

    def task_2b():
        merge("b2")

    invert(2, {2: task_2a, 6: task_2b})
    gathered("a2").wait_recv()
    turn(2, 3)
    critical(2)

    gathered("b2").wait_recv()
    lower(2, (4, 5), "b3")
    enter(3)

    def task_3():
        merge("b3")

    invert(3, {3: task_3})
    gathered("b3").wait_recv()
    turn(3, 4)
    critical(3)
    lower(3, (4, 5), "b4")

    for level in range(LEVELS - 2, -1, -1):
        pair = jnp.concatenate([tv[level, 4], tv[level, 5]], axis=1)
        if level < LEVELS - 2:
            between = jnp.concatenate([tv[level, k] for k in range(level + 1, LEVELS - 1)], axis=1)
            pair = pair - dot_full(between, zv[pl.ds(R * (level + 1), R * (LEVELS - 2 - level)), :])
        zv[pl.ds(R * level, R), :] = pair
    z_high, z_low = halves(zv[...])
    z_stack = jnp.concatenate([z_high, z_low, z_high], axis=0)

    def update(leaf, carry):
        high, low = halves(jnp.concatenate([xv[k, rows_of(leaf), :] for k in range(LEVELS - 1)], axis=1))
        change = jnp.dot(jnp.concatenate([high, high, low], axis=1), z_stack, preferred_element_type=F32)
        ab[rows_of(leaf), :] = jnp.concatenate([xv[k, rows_of(leaf), :] for k in (4, 5)], axis=1) - change
        return carry

    lax.fori_loop(0, leaves, update, 0)

    merge("b4")
    enter(4)
    invert(4, {})
    gathered("b4").wait_recv()
    weights = dot_full(iv[4], f[block(4, 5)])
    w_high, w_low = halves(weights)
    w_stack = jnp.concatenate([w_high, w_low, w_high], axis=0)

    def store(leaf):
        return pltpu.make_async_copy(ov.at[rows_of(leaf), :], o_hbm.at[rows_of(leaf), :], out_sem.at[leaf])

    def last(leaf, carry):
        high, low = halves(ab[rows_of(leaf), pl.ds(0, R)])
        change = jnp.dot(jnp.concatenate([high, high, low], axis=1), w_stack, preferred_element_type=F32)
        ov[rows_of(leaf), :] = ab[rows_of(leaf), pl.ds(R, R)] - change
        store(leaf).start()
        return carry

    lax.fori_loop(0, leaves, last, 0)
    total_ref[0, 0] = jnp.sum(log_ref[...]) / (R * R * (2**LEVELS - 1))

    for target, slot in ((rd, 0), (rs, 1), (qa, 3), (qb, 5)):
        remote(target, target, rs_send.at[slot], rs_recv.at[slot], me).wait_send()
    to_mate(A, B - A, ra, 2).wait_send()
    to_mate(B, END - B, rb, 4).wait_send()
    for name in GATHERS:
        gathered(name).wait_send()
    for name in SWAPS:
        swap(name).wait_send()
    for e in range(1, LEVELS):
        diagonal(e).wait_send()

    def finish(leaf, carry):
        store(leaf).wait()
        return carry

    lax.fori_loop(0, leaves, finish, 0)


def body(leaf_inverse, node_bases, right_sides):
    leaves, size = leaf_inverse.shape[:2]
    rows = right_sides.shape[0]
    bases = jnp.transpose(node_bases, (1, 0, 2))
    any_spec = pl.BlockSpec(memory_space=pl.ANY)
    na, nb = B - A, END - B
    shapes = [
        (leaves, size, size), (LEVELS, rows, R), (rows, R), (LEVEL_COLUMNS, rows, R), (rows, R), (rows, 2 * R),
        (COUNT, 8, 2, 8, R), (GROUP - 1, 1, 8, R), (GROUP - 1, 2, 8, R),
        (na, 8, 8, R), (nb, 8, 8, R), (na, 8, 8, R), (nb, 8, 8, R), (7, na, 8, R), (7, nb, 8, R),
        (COUNT, 8, R), (LEVELS - 1, COUNT, 8, R), (LEVELS - 1, COUNT, 8, R),
        (LEVELS - 1, R + 8, R), (LEVELS - 1, R + 8, R), (COUNT, R, R), (LEVELS, R, R),
        (LEVELS - 1, LEVEL_COLUMNS, R, R), (LEVELS - 1, LEVELS, R, R), ((LEVELS - 1) * R, 2 * R), (R, R),
        (STEP * STEP + 8, R), (STEP + 8, R), (8, R),
    ]
    dma = pltpu.SemaphoreType.DMA
    scratch = [pltpu.VMEM(shape, F32) for shape in shapes]
    scratch += [
        dma((5, leaves)), dma((leaves,)), dma((6,)), dma((6,)), dma((LEVELS - 1,)), dma((LEVELS - 1,)),
        dma((len(SWAPS),)), dma((len(SWAPS),)), dma((len(GATHERS),)), dma((len(GATHERS),)),
    ]
    solution, log_total = pl.pallas_call(
        kernel,
        out_shape=(
            jax.ShapeDtypeStruct((rows, R), F32),
            jax.ShapeDtypeStruct((1, 1), F32),
        ),
        in_specs=[any_spec] * 3,
        out_specs=(any_spec, pl.BlockSpec(memory_space=pltpu.SMEM)),
        scratch_shapes=scratch,
        compiler_params=pltpu.CompilerParams(
            collective_id=0, has_side_effects=True, vmem_limit_bytes=60 * 2**20
        ),
    )(leaf_inverse, bases, right_sides)
    return solution, log_total.reshape(())


def solution(mesh):
    return jax.shard_map(
        body,
        mesh=mesh,
        in_specs=(P("leaf", None, None), P("leaf", None, None), P("leaf", None)),
        out_specs=(P("leaf", None), P()),
        check_vma=False,
    )
```

```python
import functools

import jax
import jax.numpy as jnp
from jax import lax
from jax.experimental import pallas as pl
from jax.experimental.pallas import tpu as pltpu
from jax.sharding import PartitionSpec as P

F32 = jnp.float32
BF16 = jnp.bfloat16
MESH = pl.DeviceIdType.MESH
R = 128
LEVELS = 5
LEVEL_COLUMNS = LEVELS + 1
GROUP = 16
STEP = 16

ORDER = (
    (0, 0), (0, 1), (1, 1),
    (0, 2), (0, 3), (1, 2), (2, 2), (1, 3), (2, 3), (3, 3),
    (0, 4), (0, 5), (1, 4), (1, 5), (2, 4), (2, 5), (3, 4), (4, 4), (3, 5), (4, 5),
)
COUNT = len(ORDER)
A, B = (5, 10), (12, 20)
GATHERS = {
    "d0": (0, 1), "c0": (1, 3), "a0": (3, 5), "b0": (10, 12), "a1": (5, 7), "e1": (7, 8), "b1": (12, 14),
    "a2": (8, 10), "b2": (14, 16), "b3": (16, 18), "e3": (18, 19), "b4": (19, 20),
}
SWAPS = {"a1": (5, 10), "b1": (12, 20), "a2": (8, 10), "b2": (14, 20), "b3": (16, 20), "b4": (19, 20)}
GATHER_SLOT = {name: i for i, name in enumerate(GATHERS)}
SWAP_SLOT = {name: i for i, name in enumerate(SWAPS)}


def block(a, b):
    return ORDER.index((a, b))


def halves(v):
    high = v.astype(BF16)
    return high, (v - high.astype(F32)).astype(BF16)


def dot3(a, b):
    ah, al = halves(a)
    bh, bl = halves(b)
    return jnp.dot(
        jnp.concatenate([ah, ah, al], axis=1),
        jnp.concatenate([bh, bl, bh], axis=0),
        preferred_element_type=F32,
    )


def tdot(a, b):
    return lax.dot_general(a, b, (((0,), (0,)), ((), ())), preferred_element_type=F32)


def tdot3(a, b):
    ah, al = halves(a)
    bh, bl = halves(b)
    return tdot(jnp.concatenate([ah, ah, al], axis=0), jnp.concatenate([bh, bl, bh], axis=0))


def dot_full(a, b):
    return jnp.dot(a, b, precision=lax.Precision.HIGHEST, preferred_element_type=F32)


def thirds(v):
    high = v.astype(BF16)
    rest = v - high.astype(F32)
    middle = rest.astype(BF16)
    low = (rest - middle.astype(F32)).astype(BF16)
    return high, middle, low


def sweep(a_ref, column_ref, q_ref, log_ref, tasks):
    lane = lax.broadcasted_iota(jnp.int32, (STEP, R), 1)
    sub = lax.broadcasted_iota(jnp.int32, (STEP, R), 0)
    sub8 = lax.broadcasted_iota(jnp.int32, (8, R), 0)
    row_step = lax.broadcasted_iota(jnp.int32, (R, R), 0) // STEP
    column_step = lax.broadcasted_iota(jnp.int32, (R, R), 1) // STEP

    def pack(rows):
        groups = []
        for first in range(0, STEP, 8):
            packed = rows[first]
            for i in range(1, 8):
                packed = jnp.where(sub8 == i, rows[first + i], packed)
            groups.append(packed)
        return jnp.concatenate(groups, axis=0)

    def step(p, carry):
        for at, task in tasks.items():
            pl.when(p == at)(task)
        base = pl.multiple_of(p * STEP, STEP)
        panel = a_ref[pl.ds(base, STEP), :]
        turned = pltpu.roll(panel, lax.rem(R - base, R), axis=1)
        for j in range(STEP):
            high = (j // 8 + 1) * 8
            column_ref[pl.ds(j * STEP, high), :] = jnp.broadcast_to(turned[:high, j : j + 1], (high, R))
        q_ref[pl.ds(0, STEP), :] = jnp.where(
            lane // STEP == p, jnp.where(lane - base == sub, -1.0, 0.0), panel
        )
        rows, ratios, inverses = [], [], []
        for i in range(STEP):
            row = [column_ref[pl.ds(j * STEP + i, 8, stride=0), :] for j in range(i, STEP)]
            row.append(q_ref[pl.ds(i, 8, stride=0), :])
            row = jnp.stack(row)
            for m in range(i):
                row = row - ratios[m][i - m][None] * rows[m][i - m :]
            inverse = 1.0 / row[0]
            rows.append(row)
            inverses.append(inverse)
            ratios.append(row[: STEP - i] * inverse[None])
        v = pack([rows[i][STEP - i] for i in range(STEP)])
        w = v * pack(inverses)
        pivots = pack([rows[i][0] for i in range(STEP)])
        vh, vm, vl = thirds(v)
        wh, wm, wl = thirds(w)
        change = tdot(
            jnp.concatenate([vh, vh, vm, vh, vm, vl], axis=0),
            jnp.concatenate([wh, wm, wh, wl, wm, wh], axis=0),
        )
        a_ref[...] = jnp.where((row_step == p) | (column_step == p), 0.0, a_ref[...]) - change
        taken = jnp.log(pivots)
        log_ref[...] = log_ref[...] + taken[:8] + taken[8:]
        return carry

    lax.fori_loop(0, R // STEP, step, 0)


def kernel(
    d_hbm, u_hbm, b_hbm, o_hbm, total_ref,
    dv, uv, bv, xv, ov, ab, g, rd, rs, rta, rtb, ra, rb, ha, hb, qa, qb,
    pc, sx, rx, dx, dr, f, iv, tv, gt, zv, a_ref, column_ref, q_ref, log_ref,
    load_sem, out_sem, rs_send, rs_recv, d_send, d_recv, x_send, x_recv, g_send, g_recv,
):
    leaves = d_hbm.shape[0]
    size = d_hbm.shape[1]

    me = lax.axis_index("leaf")
    z = me // 32
    x = (me // 8) % 4
    half = x // 2
    x_in = x + half * (3 - 2 * x)
    seat = x_in * 8 + me % 8
    chip = seat // 2
    core = seat % 2
    piece = pl.multiple_of(seat * 8, 8)

    def device(other):
        xo = other // 8
        return z * 32 + (xo + half * (3 - 2 * xo)) * 8 + other % 8

    mate = me + 1 - 2 * core
    partner = (
        None,
        me + 8 * (3 - 2 * x),
        me + 32 * (1 - 2 * (z % 2)),
        me + 32 * (3 - 2 * (z % 4)),
        me + 32 * (7 - 2 * z),
    )

    barrier = pltpu.get_barrier_semaphore()

    def greet(r, carry):
        pl.semaphore_signal(barrier, inc=1, device_id=(device((seat + r) % GROUP),), device_id_type=MESH)
        return carry

    lax.fori_loop(1, GROUP, greet, 0)
    for e in range(1, LEVELS):
        pl.semaphore_signal(barrier, inc=1, device_id=(partner[e],), device_id_type=MESH)

    def rows_of(leaf):
        return pl.ds(pl.multiple_of(leaf * size, size), size)

    def load_d(leaf):
        return pltpu.make_async_copy(d_hbm.at[leaf], dv.at[leaf], load_sem.at[0, leaf])

    def load_u(leaf, first, count, slot):
        at = (pl.ds(first, count), rows_of(leaf), slice(None))
        return pltpu.make_async_copy(u_hbm.at[at], uv.at[at], load_sem.at[slot, leaf])

    def load_b(leaf):
        return pltpu.make_async_copy(b_hbm.at[rows_of(leaf), :], bv.at[rows_of(leaf), :], load_sem.at[4, leaf])

    for leaf in range(leaves):
        load_d(leaf).start()
        load_u(leaf, 0, 2, 1).start()
    for leaf in range(leaves):
        load_u(leaf, 2, 2, 2).start()
    for leaf in range(leaves):
        load_u(leaf, 4, 1, 3).start()
        load_b(leaf).start()

    def remote(source, target, send, recv, who):
        return pltpu.make_async_remote_copy(
            src_ref=source, dst_ref=target, send_sem=send, recv_sem=recv,
            device_id=(who,), device_id_type=MESH,
        )

    def columns_of(columns):
        top = min(columns[-1], LEVELS - 1)
        u = [uv[j] for j in range(top + 1)]
        have = [u[k] if k < LEVELS else bv[...] for k in columns]
        high, low = halves(jnp.concatenate(have, axis=1))
        got = []
        for leaf in range(leaves):
            at = slice(size * leaf, size * (leaf + 1))
            d_high, d_low = halves(dv[leaf])
            got.append(
                jnp.dot(
                    jnp.concatenate([d_high, d_high, d_low], axis=1),
                    jnp.concatenate([high[at], low[at], high[at]], axis=0),
                    preferred_element_type=F32,
                )
            )
        got = jnp.concatenate(got, axis=0)
        products = tdot3(jnp.concatenate(u, axis=1), got)
        for i, k in enumerate(columns):
            xv[k] = got[:, R * i : R * (i + 1)]
            for j in range(min(k, LEVELS - 1) + 1):
                g[block(j, k)] = products[R * j : R * (j + 1), R * i : R * (i + 1)].reshape(8, 2, 8, R)

    def scatter(first, count, target, slot):
        def one(r, carry):
            other = (seat + r) % GROUP
            remote(
                g.at[pl.ds(first, count), other // 2, other % 2], target.at[r - 1],
                rs_send.at[slot], rs_recv.at[slot], device(other),
            ).start()
            return carry

        lax.fori_loop(1, GROUP, one, 0)

    def scattered(first, count, target, slot):
        remote(target, target, rs_send.at[slot], rs_recv.at[slot], me).wait_recv()
        kept = g[pl.ds(first, count), chip, core]
        for r in range(GROUP - 1):
            kept = kept + target[r]
        pc[pl.ds(first, count)] = kept

    def to_mate(blocks, target, slot):
        first, last = blocks
        return remote(
            g.at[pl.ds(first, last - first), pl.ds(0, 8), 1 - core], target, rs_send.at[slot], rs_recv.at[slot], mate
        )

    def scatter_chips(blocks, from_mate, summed, target, slot):
        first, last = blocks
        to_mate(blocks, from_mate, slot - 1).wait_recv()

        def add(i, carry):
            summed[i] = g[i + first, :, core] + from_mate[i]
            return carry

        lax.fori_loop(0, last - first, add, 0)

        def one(r, carry):
            other = (chip + r) % 8
            remote(
                summed.at[pl.ds(0, last - first), other], target.at[r - 1],
                rs_send.at[slot], rs_recv.at[slot], device(other * 2 + core),
            ).start()
            return carry

        lax.fori_loop(1, 8, one, 0)

    def scattered_chips(blocks, summed, target, slot):
        first, last = blocks
        remote(target, target, rs_send.at[slot], rs_recv.at[slot], me).wait_recv()
        kept = summed[:, chip]
        for r in range(7):
            kept = kept + target[r]
        pc[pl.ds(first, last - first)] = kept

    def gather(name):
        first, last = GATHERS[name]
        slot = GATHER_SLOT[name]
        f[pl.ds(first, last - first), pl.ds(piece, 8), :] = pc[pl.ds(first, last - first)]

        def one(r, carry):
            other = (seat + r) % GROUP
            remote(
                pc.at[pl.ds(first, last - first)],
                f.at[pl.ds(first, last - first), pl.ds(piece, 8), :],
                g_send.at[slot], g_recv.at[slot], device(other),
            ).start()
            return carry

        lax.fori_loop(1, GROUP, one, 0)

    def gathered(name):
        first, last = GATHERS[name]
        slot = GATHER_SLOT[name]
        ref = f.at[pl.ds(first, last - first), pl.ds(0, 120), :]
        return remote(ref, ref, g_send.at[slot], g_recv.at[slot], me)

    def diagonal(e):
        return remote(dx.at[e - 1], dr.at[e - 1], d_send.at[e - 1], d_recv.at[e - 1], partner[e])

    def swap(name):
        first, last = SWAPS[name]
        e = int(name[1])
        slot = SWAP_SLOT[name]
        at = pl.ds(first, last - first)
        return remote(sx.at[e - 1, at], rx.at[e - 1, at], x_send.at[slot], x_recv.at[slot], partner[e])

    def whole(a, b):
        return f[block(a, b)]

    def turn(level, k):
        gt[level, k] = whole(level, k).T

    def critical(level):
        e = level + 1
        ratio = dot_full(iv[level], whole(level, e))
        tv[level, e] = ratio
        dx[e - 1, pl.ds(0, R), :] = whole(e, e) - dot_full(gt[level, e], ratio)
        dx[e - 1, pl.ds(R, 8), :] = log_ref[...]
        diagonal(e).start()

    def lower(level, columns, name):
        e = level + 1
        first, last = SWAPS[name]
        fresh = [k for k in columns if k != e]
        ratio = dot3(iv[level], jnp.concatenate([whole(level, k) for k in fresh], axis=1))
        for i, k in enumerate(fresh):
            tv[level, k] = ratio[:, R * i : R * (i + 1)]
            if k < LEVELS:
                turn(level, k)
        ends = [r for r in range(e, LEVELS) if r <= columns[-1]]
        left = jnp.concatenate([gt[level, r, pl.ds(piece, 8), :] for r in ends], axis=0)
        down = dot3(left, ratio)
        for at in range(first, last):
            r, k = ORDER[at]
            i = fresh.index(k)
            sx[e - 1, at] = pc[at] - down[8 * (r - e) : 8 * (r - e) + 8, R * i : R * (i + 1)]
        swap(name).start()

    def merge(name, *sets):
        first, last = SWAPS[name]
        e = int(name[1])
        swap(name).wait_recv()
        at = pl.ds(first, last - first)
        pc[at] = sx[e - 1, at] + rx[e - 1, at]
        for each in sets:
            gather(each)

    def enter(e):
        diagonal(e).wait_recv()
        a_ref[...] = dx[e - 1, pl.ds(0, R), :] + dr[e - 1, pl.ds(0, R), :] + eye
        log_ref[...] = dx[e - 1, pl.ds(R, 8), :] + dr[e - 1, pl.ds(R, 8), :]

    def invert(level, tasks):
        sweep(a_ref, column_ref, q_ref, log_ref, tasks)
        iv[level] = -a_ref[...]

    eye = (
        lax.broadcasted_iota(jnp.int32, (R, R), 0) == lax.broadcasted_iota(jnp.int32, (R, R), 1)
    ).astype(F32)

    for leaf in range(leaves):
        load_d(leaf).wait()
        load_u(leaf, 0, 2, 1).wait()
    columns_of((0, 1))
    pl.semaphore_wait(barrier, GROUP - 1 + LEVELS - 1)
    scatter(0, 1, rd, 0)
    scatter(1, 2, rs, 1)
    for leaf in range(leaves):
        load_u(leaf, 2, 2, 2).wait()
    columns_of((2, 3))
    scatter(3, 2, rta, 2)
    to_mate(A, ra, 4).start()
    scattered(0, 1, rd, 0)
    gather("d0")
    for leaf in range(leaves):
        load_u(leaf, 4, 1, 3).wait()
        load_b(leaf).wait()
    columns_of((4, 5))
    scatter(10, 2, rtb, 3)
    to_mate(B, rb, 6).start()
    scattered(1, 2, rs, 1)
    gather("c0")
    scatter_chips(A, ra, ha, qa, 5)
    gathered("d0").wait_recv()
    a_ref[...] = whole(0, 0) + eye
    log_ref[...] = jnp.zeros((8, R), F32)

    def task_0a():
        scattered(3, 2, rta, 2)
        gather("a0")

    def task_0b():
        scatter_chips(B, rb, hb, qb, 7)

    def task_0c():
        scattered(10, 2, rtb, 3)
        gather("b0")

    invert(0, {1: task_0a, 3: task_0b, 6: task_0c})
    gathered("c0").wait_recv()
    turn(0, 1)
    critical(0)
    scattered_chips(A, ha, qa, 5)
    gathered("a0").wait_recv()
    lower(0, (2, 3), "a1")

    enter(1)
    merge("a1", "a1", "e1")

    def task_1a():
        scattered_chips(B, hb, qb, 7)
        gathered("b0").wait_recv()
        lower(0, (4, 5), "b1")

    def task_1b():
        merge("b1", "b1")

    invert(1, {1: task_1a, 5: task_1b})
    gathered("a1").wait_recv()
    turn(1, 2)
    critical(1)
    gathered("e1").wait_recv()
    lower(1, (2, 3), "a2")

    enter(2)
    merge("a2", "a2")

    def task_2a():
        gathered("b1").wait_recv()
        lower(1, (4, 5), "b2")

    def task_2b():
        merge("b2", "b2")

    invert(2, {1: task_2a, 5: task_2b})
    gathered("a2").wait_recv()
    turn(2, 3)
    critical(2)
    gathered("b2").wait_recv()
    lower(2, (4, 5), "b3")

    enter(3)

    def task_3():
        merge("b3", "b3", "e3")

    invert(3, {2: task_3})
    gathered("b3").wait_recv()
    turn(3, 4)
    critical(3)
    gathered("e3").wait_recv()
    lower(3, (4, 5), "b4")

    for level in range(LEVELS - 2, -1, -1):
        pair = jnp.concatenate([tv[level, 4], tv[level, 5]], axis=1)
        if level < LEVELS - 2:
            between = jnp.concatenate([tv[level, k] for k in range(level + 1, LEVELS - 1)], axis=1)
            pair = pair - dot3(between, zv[pl.ds(R * (level + 1), R * (LEVELS - 2 - level)), :])
        zv[pl.ds(R * level, R), :] = pair
    z_high, z_low = halves(zv[...])
    z_stack = jnp.concatenate([z_high, z_low, z_high], axis=0)

    high, low = halves(jnp.concatenate([xv[k] for k in range(LEVELS - 1)], axis=1))
    change = jnp.dot(jnp.concatenate([high, high, low], axis=1), z_stack, preferred_element_type=F32)
    ab[...] = jnp.concatenate([xv[k] for k in (4, 5)], axis=1) - change

    merge("b4", "b4")
    enter(4)
    invert(4, {})
    gathered("b4").wait_recv()
    weights = dot_full(iv[4], whole(4, 5))
    w_high, w_low = halves(weights)
    w_stack = jnp.concatenate([w_high, w_low, w_high], axis=0)

    part = 2 * size

    def store(i):
        at = pl.ds(i * part, part)
        return pltpu.make_async_copy(ov.at[at, :], o_hbm.at[at, :], out_sem.at[i])

    for i in range(leaves // 2):
        at = pl.ds(i * part, part)
        high, low = halves(ab[at, pl.ds(0, R)])
        change = jnp.dot(jnp.concatenate([high, high, low], axis=1), w_stack, preferred_element_type=F32)
        ov[at, :] = ab[at, pl.ds(R, R)] - change
        store(i).start()
    total_ref[0, 0] = jnp.sum(log_ref[...]) / (R * R * (2**LEVELS - 1))

    for target, slot in ((rd, 0), (rs, 1), (rta, 2), (rtb, 3), (qa, 5), (qb, 7)):
        remote(target, target, rs_send.at[slot], rs_recv.at[slot], me).wait_send()
    to_mate(A, ra, 4).wait_send()
    to_mate(B, rb, 6).wait_send()
    for name in GATHERS:
        gathered(name).wait_send()
    for name in SWAPS:
        swap(name).wait_send()
    for e in range(1, LEVELS):
        diagonal(e).wait_send()

    for i in range(leaves // 2):
        store(i).wait()


def body(leaf_inverse, node_bases, right_sides):
    leaves, size = leaf_inverse.shape[:2]
    rows = right_sides.shape[0]
    bases = jnp.transpose(node_bases, (1, 0, 2))
    any_spec = pl.BlockSpec(memory_space=pl.ANY)
    na, nb = A[1] - A[0], B[1] - B[0]
    shapes = [
        (leaves, size, size), (LEVELS, rows, R), (rows, R), (LEVEL_COLUMNS, rows, R), (rows, R), (rows, 2 * R),
        (COUNT, 8, 2, 8, R), (GROUP - 1, 1, 8, R), (GROUP - 1, 2, 8, R), (GROUP - 1, 2, 8, R), (GROUP - 1, 2, 8, R),
        (na, 8, 8, R), (nb, 8, 8, R), (na, 8, 8, R), (nb, 8, 8, R), (7, na, 8, R), (7, nb, 8, R),
        (COUNT, 8, R), (LEVELS - 1, COUNT, 8, R), (LEVELS - 1, COUNT, 8, R),
        (LEVELS - 1, R + 8, R), (LEVELS - 1, R + 8, R), (COUNT, R, R), (LEVELS, R, R),
        (LEVELS - 1, LEVEL_COLUMNS, R, R), (LEVELS - 1, LEVELS, R, R), ((LEVELS - 1) * R, 2 * R), (R, R),
        (STEP * STEP + 8, R), (STEP + 8, R), (8, R),
    ]
    dma = pltpu.SemaphoreType.DMA
    scratch = [pltpu.VMEM(shape, F32) for shape in shapes]
    scratch += [
        dma((5, leaves)), dma((leaves,)), dma((8,)), dma((8,)), dma((LEVELS - 1,)), dma((LEVELS - 1,)),
        dma((len(SWAPS),)), dma((len(SWAPS),)), dma((len(GATHERS),)), dma((len(GATHERS),)),
    ]
    solution, log_total = pl.pallas_call(
        kernel,
        out_shape=(
            jax.ShapeDtypeStruct((rows, R), F32),
            jax.ShapeDtypeStruct((1, 1), F32),
        ),
        in_specs=[any_spec] * 3,
        out_specs=(any_spec, pl.BlockSpec(memory_space=pltpu.SMEM)),
        scratch_shapes=scratch,
        compiler_params=pltpu.CompilerParams(
            collective_id=0, has_side_effects=True, vmem_limit_bytes=60 * 2**20
        ),
    )(leaf_inverse, bases, right_sides)
    return solution, log_total.reshape(())


def solution(mesh):
    return jax.shard_map(
        body,
        mesh=mesh,
        in_specs=(P("leaf", None, None), P("leaf", None, None), P("leaf", None)),
        out_specs=(P("leaf", None), P()),
        check_vma=False,
    )
```

```python
import functools

import jax
import jax.numpy as jnp
from jax import lax
from jax.experimental import pallas as pl
from jax.experimental.pallas import tpu as pltpu
from jax.sharding import PartitionSpec as P

F32 = jnp.float32
BF16 = jnp.bfloat16
MESH = pl.DeviceIdType.MESH
R = 128
LEVELS = 5
LEVEL_COLUMNS = LEVELS + 1
GROUP = 16
STEP = 16

ORDER = (
    (0, 0), (0, 1), (1, 1),
    (0, 2), (0, 3), (1, 2), (2, 2), (1, 3), (2, 3), (3, 3),
    (0, 4), (0, 5), (1, 4), (1, 5), (2, 4), (2, 5), (3, 4), (4, 4), (3, 5), (4, 5),
)
COUNT = len(ORDER)
A, B = (5, 10), (12, 20)
GATHERS = {
    "d0": (0, 1), "c0": (1, 3), "a0": (3, 5), "b0": (10, 12), "a1": (5, 7), "e1": (7, 8), "b1": (12, 14),
    "a2": (8, 10), "b2": (14, 16), "b3": (16, 18), "e3": (18, 19), "b4": (19, 20),
}
SWAPS = {"a1": (5, 10), "b1": (12, 20), "a2": (8, 10), "b2": (14, 20), "b3": (16, 20), "b4": (19, 20)}
GATHER_SLOT = {name: i for i, name in enumerate(GATHERS)}
SWAP_SLOT = {name: i for i, name in enumerate(SWAPS)}


def block(a, b):
    return ORDER.index((a, b))


def halves(v):
    high = v.astype(BF16)
    return high, (v - high.astype(F32)).astype(BF16)


def dot3(a, b):
    ah, al = halves(a)
    bh, bl = halves(b)
    return jnp.dot(
        jnp.concatenate([ah, ah, al], axis=1),
        jnp.concatenate([bh, bl, bh], axis=0),
        preferred_element_type=F32,
    )


def tdot(a, b):
    return lax.dot_general(a, b, (((0,), (0,)), ((), ())), preferred_element_type=F32)


def tdot3(a, b):
    ah, al = halves(a)
    bh, bl = halves(b)
    return tdot(jnp.concatenate([ah, ah, al], axis=0), jnp.concatenate([bh, bl, bh], axis=0))


def dot_full(a, b):
    return jnp.dot(a, b, precision=lax.Precision.HIGHEST, preferred_element_type=F32)


def thirds(v):
    high = v.astype(BF16)
    rest = v - high.astype(F32)
    middle = rest.astype(BF16)
    low = (rest - middle.astype(F32)).astype(BF16)
    return high, middle, low


def sweep(a_ref, column_ref, q_ref, log_ref, tasks):
    lane = lax.broadcasted_iota(jnp.int32, (STEP, R), 1)
    sub = lax.broadcasted_iota(jnp.int32, (STEP, R), 0)
    sub8 = lax.broadcasted_iota(jnp.int32, (8, R), 0)
    row_step = lax.broadcasted_iota(jnp.int32, (R, R), 0) // STEP
    column_step = lax.broadcasted_iota(jnp.int32, (R, R), 1) // STEP

    def pack(rows):
        groups = []
        for first in range(0, STEP, 8):
            packed = rows[first]
            for i in range(1, 8):
                packed = jnp.where(sub8 == i, rows[first + i], packed)
            groups.append(packed)
        return jnp.concatenate(groups, axis=0)

    def step(p, carry):
        for at, task in tasks.items():
            pl.when(p == at)(task)
        base = pl.multiple_of(p * STEP, STEP)
        panel = a_ref[pl.ds(base, STEP), :]
        turned = pltpu.roll(panel, lax.rem(R - base, R), axis=1)
        for j in range(STEP):
            high = (j // 8 + 1) * 8
            column_ref[pl.ds(j * STEP, high), :] = jnp.broadcast_to(turned[:high, j : j + 1], (high, R))
        q_ref[pl.ds(0, STEP), :] = jnp.where(
            lane // STEP == p, jnp.where(lane - base == sub, -1.0, 0.0), panel
        )
        rows, ratios, inverses = [], [], []
        for i in range(STEP):
            row = [column_ref[pl.ds(j * STEP + i, 8, stride=0), :] for j in range(i, STEP)]
            row.append(q_ref[pl.ds(i, 8, stride=0), :])
            row = jnp.stack(row)
            for m in range(i):
                row = row - ratios[m][i - m][None] * rows[m][i - m :]
            inverse = 1.0 / row[0]
            rows.append(row)
            inverses.append(inverse)
            ratios.append(row[: STEP - i] * inverse[None])
        v = pack([rows[i][STEP - i] for i in range(STEP)])
        w = v * pack(inverses)
        pivots = pack([rows[i][0] for i in range(STEP)])
        vh, vm, vl = thirds(v)
        wh, wm, wl = thirds(w)
        change = tdot(
            jnp.concatenate([vh, vh, vm, vh, vm, vl], axis=0),
            jnp.concatenate([wh, wm, wh, wl, wm, wh], axis=0),
        )
        a_ref[...] = jnp.where((row_step == p) | (column_step == p), 0.0, a_ref[...]) - change
        taken = jnp.log(pivots)
        log_ref[...] = log_ref[...] + taken[:8] + taken[8:]
        return carry

    lax.fori_loop(0, R // STEP, step, 0)


def kernel(
    d_hbm, u_hbm, b_hbm, ab_hbm, weights_ref, total_ref,
    dv, uv, bv, xv, ab, g, rd, rs, rta, rtb, ra, rb, ha, hb, qa, qb,
    pc, sx, rx, dx, dr, f, iv, tv, gt, zv, a_ref, column_ref, q_ref, log_ref,
    load_sem, out_sem, rs_send, rs_recv, d_send, d_recv, x_send, x_recv, g_send, g_recv,
):
    leaves = d_hbm.shape[0]
    size = d_hbm.shape[1]

    me = lax.axis_index("leaf")
    z = me // 32
    x = (me // 8) % 4
    half = x // 2
    x_in = x + half * (3 - 2 * x)
    seat = x_in * 8 + me % 8
    chip = seat // 2
    core = seat % 2
    piece = pl.multiple_of(seat * 8, 8)

    def device(other):
        xo = other // 8
        return z * 32 + (xo + half * (3 - 2 * xo)) * 8 + other % 8

    mate = me + 1 - 2 * core
    partner = (
        None,
        me + 8 * (3 - 2 * x),
        me + 32 * (1 - 2 * (z % 2)),
        me + 32 * (3 - 2 * (z % 4)),
        me + 32 * (7 - 2 * z),
    )

    barrier = pltpu.get_barrier_semaphore()

    def greet(r, carry):
        pl.semaphore_signal(barrier, inc=1, device_id=(device((seat + r) % GROUP),), device_id_type=MESH)
        return carry

    lax.fori_loop(1, GROUP, greet, 0)
    for e in range(1, LEVELS):
        pl.semaphore_signal(barrier, inc=1, device_id=(partner[e],), device_id_type=MESH)

    def rows_of(leaf):
        return pl.ds(pl.multiple_of(leaf * size, size), size)

    def load_d(leaf):
        return pltpu.make_async_copy(d_hbm.at[leaf], dv.at[leaf], load_sem.at[0, leaf])

    def load_u(leaf, first, count, slot):
        at = (pl.ds(first, count), rows_of(leaf), slice(None))
        return pltpu.make_async_copy(u_hbm.at[at], uv.at[at], load_sem.at[slot, leaf])

    def load_b(leaf):
        return pltpu.make_async_copy(b_hbm.at[rows_of(leaf), :], bv.at[rows_of(leaf), :], load_sem.at[4, leaf])

    for leaf in range(leaves):
        load_d(leaf).start()
        load_u(leaf, 0, 2, 1).start()
    for leaf in range(leaves):
        load_u(leaf, 2, 2, 2).start()
    for leaf in range(leaves):
        load_u(leaf, 4, 1, 3).start()
        load_b(leaf).start()

    def remote(source, target, send, recv, who):
        return pltpu.make_async_remote_copy(
            src_ref=source, dst_ref=target, send_sem=send, recv_sem=recv,
            device_id=(who,), device_id_type=MESH,
        )

    def columns_of(columns):
        top = min(columns[-1], LEVELS - 1)
        u = [uv[j] for j in range(top + 1)]
        have = [u[k] if k < LEVELS else bv[...] for k in columns]
        high, low = halves(jnp.concatenate(have, axis=1))
        got = []
        for leaf in range(leaves):
            at = slice(size * leaf, size * (leaf + 1))
            d_high, d_low = halves(dv[leaf])
            got.append(
                jnp.dot(
                    jnp.concatenate([d_high, d_high, d_low], axis=1),
                    jnp.concatenate([high[at], low[at], high[at]], axis=0),
                    preferred_element_type=F32,
                )
            )
        got = jnp.concatenate(got, axis=0)
        products = tdot3(jnp.concatenate(u, axis=1), got)
        for i, k in enumerate(columns):
            xv[k] = got[:, R * i : R * (i + 1)]
            for j in range(min(k, LEVELS - 1) + 1):
                g[block(j, k)] = products[R * j : R * (j + 1), R * i : R * (i + 1)].reshape(8, 2, 8, R)

    def scatter(first, count, target, slot):
        def one(r, carry):
            other = (seat + r) % GROUP
            remote(
                g.at[pl.ds(first, count), other // 2, other % 2], target.at[r - 1],
                rs_send.at[slot], rs_recv.at[slot], device(other),
            ).start()
            return carry

        lax.fori_loop(1, GROUP, one, 0, unroll=3)

    def scattered(first, count, target, slot):
        remote(target, target, rs_send.at[slot], rs_recv.at[slot], me).wait_recv()
        kept = g[pl.ds(first, count), chip, core]
        for r in range(GROUP - 1):
            kept = kept + target[r]
        pc[pl.ds(first, count)] = kept

    def to_mate(blocks, target, slot):
        first, last = blocks
        return remote(
            g.at[pl.ds(first, last - first), pl.ds(0, 8), 1 - core], target, rs_send.at[slot], rs_recv.at[slot], mate
        )

    def scatter_chips(blocks, from_mate, summed, target, slot):
        first, last = blocks
        to_mate(blocks, from_mate, slot - 1).wait_recv()

        def add(i, carry):
            summed[i] = g[i + first, :, core] + from_mate[i]
            return carry

        lax.fori_loop(0, last - first, add, 0)

        def one(r, carry):
            other = (chip + r) % 8
            remote(
                summed.at[pl.ds(0, last - first), other], target.at[r - 1],
                rs_send.at[slot], rs_recv.at[slot], device(other * 2 + core),
            ).start()
            return carry

        lax.fori_loop(1, 8, one, 0, unroll=True)

    def scattered_chips(blocks, summed, target, slot):
        first, last = blocks
        remote(target, target, rs_send.at[slot], rs_recv.at[slot], me).wait_recv()
        kept = summed[:, chip]
        for r in range(7):
            kept = kept + target[r]
        pc[pl.ds(first, last - first)] = kept

    def gather(name):
        first, last = GATHERS[name]
        slot = GATHER_SLOT[name]
        f[pl.ds(first, last - first), pl.ds(piece, 8), :] = pc[pl.ds(first, last - first)]

        def one(r, carry):
            other = (seat + r) % GROUP
            remote(
                pc.at[pl.ds(first, last - first)],
                f.at[pl.ds(first, last - first), pl.ds(piece, 8), :],
                g_send.at[slot], g_recv.at[slot], device(other),
            ).start()
            return carry

        lax.fori_loop(1, GROUP, one, 0, unroll=3)

    def gathered(name):
        first, last = GATHERS[name]
        slot = GATHER_SLOT[name]
        ref = f.at[pl.ds(first, last - first), pl.ds(0, 120), :]
        return remote(ref, ref, g_send.at[slot], g_recv.at[slot], me)

    def diagonal(e):
        return remote(dx.at[e - 1], dr.at[e - 1], d_send.at[e - 1], d_recv.at[e - 1], partner[e])

    def swap(name):
        first, last = SWAPS[name]
        e = int(name[1])
        slot = SWAP_SLOT[name]
        at = pl.ds(first, last - first)
        return remote(sx.at[e - 1, at], rx.at[e - 1, at], x_send.at[slot], x_recv.at[slot], partner[e])

    def whole(a, b):
        return f[block(a, b)]

    def turn(level, k):
        gt[level, k] = whole(level, k).T

    def critical(level):
        e = level + 1
        ratio = dot_full(iv[level], whole(level, e))
        tv[level, e] = ratio
        dx[e - 1, pl.ds(0, R), :] = whole(e, e) - dot_full(gt[level, e], ratio)
        dx[e - 1, pl.ds(R, 8), :] = log_ref[...]
        diagonal(e).start()

    def lower(level, columns, name):
        e = level + 1
        first, last = SWAPS[name]
        fresh = [k for k in columns if k != e]
        ratio = dot3(iv[level], jnp.concatenate([whole(level, k) for k in fresh], axis=1))
        for i, k in enumerate(fresh):
            tv[level, k] = ratio[:, R * i : R * (i + 1)]
            if k < LEVELS:
                turn(level, k)
        ends = [r for r in range(e, LEVELS) if r <= columns[-1]]
        left = jnp.concatenate([gt[level, r, pl.ds(piece, 8), :] for r in ends], axis=0)
        down = dot3(left, ratio)
        for at in range(first, last):
            r, k = ORDER[at]
            i = fresh.index(k)
            sx[e - 1, at] = pc[at] - down[8 * (r - e) : 8 * (r - e) + 8, R * i : R * (i + 1)]
        swap(name).start()

    def merge(name, *sets):
        first, last = SWAPS[name]
        e = int(name[1])
        swap(name).wait_recv()
        at = pl.ds(first, last - first)
        pc[at] = sx[e - 1, at] + rx[e - 1, at]
        for each in sets:
            gather(each)

    def enter(e):
        diagonal(e).wait_recv()
        a_ref[...] = dx[e - 1, pl.ds(0, R), :] + dr[e - 1, pl.ds(0, R), :] + eye
        log_ref[...] = dx[e - 1, pl.ds(R, 8), :] + dr[e - 1, pl.ds(R, 8), :]

    def invert(level, tasks):
        sweep(a_ref, column_ref, q_ref, log_ref, tasks)
        iv[level] = -a_ref[...]

    eye = (
        lax.broadcasted_iota(jnp.int32, (R, R), 0) == lax.broadcasted_iota(jnp.int32, (R, R), 1)
    ).astype(F32)

    for leaf in range(leaves):
        load_d(leaf).wait()
        load_u(leaf, 0, 2, 1).wait()
    columns_of((0, 1))
    pl.semaphore_wait(barrier, GROUP - 1 + LEVELS - 1)
    scatter(0, 1, rd, 0)
    scatter(1, 2, rs, 1)
    for leaf in range(leaves):
        load_u(leaf, 2, 2, 2).wait()
    columns_of((2, 3))
    scatter(3, 2, rta, 2)
    to_mate(A, ra, 4).start()
    scattered(0, 1, rd, 0)
    gather("d0")
    for leaf in range(leaves):
        load_u(leaf, 4, 1, 3).wait()
        load_b(leaf).wait()
    columns_of((4, 5))
    scatter(10, 2, rtb, 3)
    to_mate(B, rb, 6).start()
    scattered(1, 2, rs, 1)
    gather("c0")
    scatter_chips(A, ra, ha, qa, 5)
    gathered("d0").wait_recv()
    a_ref[...] = whole(0, 0) + eye
    log_ref[...] = jnp.zeros((8, R), F32)

    def task_0a():
        scattered(3, 2, rta, 2)
        gather("a0")

    def task_0b():
        scatter_chips(B, rb, hb, qb, 7)

    def task_0c():
        scattered(10, 2, rtb, 3)
        gather("b0")

    invert(0, {1: task_0a, 3: task_0b, 5: task_0c})
    gathered("c0").wait_recv()
    turn(0, 1)
    critical(0)
    scattered_chips(A, ha, qa, 5)
    gathered("a0").wait_recv()
    lower(0, (2, 3), "a1")
    scattered_chips(B, hb, qb, 7)
    gathered("b0").wait_recv()
    lower(0, (4, 5), "b1")

    enter(1)
    merge("a1", "a1", "e1")

    def task_1():
        merge("b1", "b1")

    invert(1, {3: task_1})
    gathered("a1").wait_recv()
    turn(1, 2)
    critical(1)
    gathered("e1").wait_recv()
    lower(1, (2, 3), "a2")
    gathered("b1").wait_recv()
    lower(1, (4, 5), "b2")

    enter(2)
    merge("a2", "a2")

    def task_2():
        merge("b2", "b2")

    invert(2, {3: task_2})
    gathered("a2").wait_recv()
    turn(2, 3)
    critical(2)
    gathered("b2").wait_recv()
    lower(2, (4, 5), "b3")

    enter(3)
    merge("b3", "b3", "e3")
    invert(3, {})
    gathered("b3").wait_recv()
    turn(3, 4)
    critical(3)
    gathered("e3").wait_recv()
    lower(3, (4, 5), "b4")

    for level in range(LEVELS - 2, -1, -1):
        pair = jnp.concatenate([tv[level, 4], tv[level, 5]], axis=1)
        if level < LEVELS - 2:
            between = jnp.concatenate([tv[level, k] for k in range(level + 1, LEVELS - 1)], axis=1)
            pair = pair - dot3(between, zv[pl.ds(R * (level + 1), R * (LEVELS - 2 - level)), :])
        zv[pl.ds(R * level, R), :] = pair
    z_high, z_low = halves(zv[...])
    z_stack = jnp.concatenate([z_high, z_low, z_high], axis=0)

    high, low = halves(jnp.concatenate([xv[k] for k in range(LEVELS - 1)], axis=1))
    change = jnp.dot(jnp.concatenate([high, high, low], axis=1), z_stack, preferred_element_type=F32)
    ab[...] = jnp.concatenate([xv[k] for k in (4, 5)], axis=1) - change
    leave = pltpu.make_async_copy(ab, ab_hbm, out_sem)
    leave.start()

    merge("b4", "b4")
    enter(4)
    invert(4, {})
    gathered("b4").wait_recv()
    weights_ref[...] = dot_full(iv[4], whole(4, 5))
    total_ref[0, 0] = jnp.sum(log_ref[...]) / (R * R * (2**LEVELS - 1))

    for target, slot in ((rd, 0), (rs, 1), (rta, 2), (rtb, 3), (qa, 5), (qb, 7)):
        remote(target, target, rs_send.at[slot], rs_recv.at[slot], me).wait_send()
    to_mate(A, ra, 4).wait_send()
    to_mate(B, rb, 6).wait_send()
    for name in GATHERS:
        gathered(name).wait_send()
    for name in SWAPS:
        swap(name).wait_send()
    for e in range(1, LEVELS):
        diagonal(e).wait_send()

    leave.wait()


def finish(columns_ref, weights_ref, total_ref, o_ref, log_ref):
    o_ref[...] = columns_ref[:, R:] - dot3(columns_ref[:, :R], weights_ref[...])

    @pl.when(pl.program_id(0) == 0)
    def _():
        log_ref[0, 0] = total_ref[0, 0]


def body(leaf_inverse, node_bases, right_sides):
    leaves, size = leaf_inverse.shape[:2]
    rows = right_sides.shape[0]
    bases = jnp.transpose(node_bases, (1, 0, 2))
    any_spec = pl.BlockSpec(memory_space=pl.ANY)
    na, nb = A[1] - A[0], B[1] - B[0]
    shapes = [
        (leaves, size, size), (LEVELS, rows, R), (rows, R), (LEVEL_COLUMNS, rows, R), (rows, 2 * R),
        (COUNT, 8, 2, 8, R), (GROUP - 1, 1, 8, R), (GROUP - 1, 2, 8, R), (GROUP - 1, 2, 8, R), (GROUP - 1, 2, 8, R),
        (na, 8, 8, R), (nb, 8, 8, R), (na, 8, 8, R), (nb, 8, 8, R), (7, na, 8, R), (7, nb, 8, R),
        (COUNT, 8, R), (LEVELS - 1, COUNT, 8, R), (LEVELS - 1, COUNT, 8, R),
        (LEVELS - 1, R + 8, R), (LEVELS - 1, R + 8, R), (COUNT, R, R), (LEVELS, R, R),
        (LEVELS - 1, LEVEL_COLUMNS, R, R), (LEVELS - 1, LEVELS, R, R), ((LEVELS - 1) * R, 2 * R), (R, R),
        (STEP * STEP + 8, R), (STEP + 8, R), (8, R),
    ]
    dma = pltpu.SemaphoreType.DMA
    scratch = [pltpu.VMEM(shape, F32) for shape in shapes]
    scratch += [
        dma((5, leaves)), dma(()), dma((8,)), dma((8,)), dma((LEVELS - 1,)), dma((LEVELS - 1,)),
        dma((len(SWAPS),)), dma((len(SWAPS),)), dma((len(GATHERS),)), dma((len(GATHERS),)),
    ]
    smem = pl.BlockSpec(memory_space=pltpu.SMEM)
    columns, weights, total = pl.pallas_call(
        kernel,
        out_shape=(
            jax.ShapeDtypeStruct((rows, 2 * R), F32),
            jax.ShapeDtypeStruct((R, R), F32),
            jax.ShapeDtypeStruct((1, 1), F32),
        ),
        in_specs=[any_spec] * 3,
        out_specs=(any_spec, pl.BlockSpec(memory_space=pltpu.VMEM), smem),
        scratch_shapes=scratch,
        compiler_params=pltpu.CompilerParams(
            collective_id=0, has_side_effects=True, vmem_limit_bytes=60 * 2**20
        ),
    )(leaf_inverse, bases, right_sides)
    part = rows // 4
    solution, log_total = pl.pallas_call(
        finish,
        grid=(4,),
        out_shape=(
            jax.ShapeDtypeStruct((rows, R), F32),
            jax.ShapeDtypeStruct((1, 1), F32),
        ),
        in_specs=[
            pl.BlockSpec((part, 2 * R), lambda i: (i, 0)),
            pl.BlockSpec((R, R), lambda i: (0, 0)),
            smem,
        ],
        out_specs=(pl.BlockSpec((part, R), lambda i: (i, 0)), smem),
    )(columns, weights, total)
    return solution, log_total.reshape(())


def solution(mesh):
    return jax.shard_map(
        body,
        mesh=mesh,
        in_specs=(P("leaf", None, None), P("leaf", None, None), P("leaf", None)),
        out_specs=(P("leaf", None), P()),
        check_vma=False,
    )
```

```python
import functools

import jax
import jax.numpy as jnp
from jax import lax
from jax.experimental import pallas as pl
from jax.experimental.pallas import tpu as pltpu
from jax.sharding import PartitionSpec as P

F32 = jnp.float32
BF16 = jnp.bfloat16
MESH = pl.DeviceIdType.MESH
R = 128
LEVELS = 5
LEVEL_COLUMNS = LEVELS + 1
GROUP = 16
STEP = 16

ORDER = (
    (0, 0), (0, 1), (1, 1),
    (0, 2), (0, 3), (1, 2), (2, 2), (1, 3), (2, 3), (3, 3),
    (0, 4), (0, 5), (1, 4), (1, 5), (2, 4), (2, 5), (3, 4), (4, 4), (3, 5), (4, 5),
)
COUNT = len(ORDER)
A, B = (5, 10), (12, 20)
GATHERS = {
    "d0": (0, 1), "c0": (1, 3), "a0": (3, 5), "b0": (10, 12), "a1": (5, 7), "e1": (7, 8), "b1": (12, 14),
    "a2": (8, 10), "b2": (14, 16), "b3": (16, 18), "e3": (18, 19), "b4": (19, 20),
}
SWAPS = {"a1": (5, 10), "b1": (12, 20), "a2": (8, 10), "b2": (14, 20), "b3": (16, 20), "b4": (19, 20)}
GATHER_SLOT = {name: i for i, name in enumerate(GATHERS)}
SWAP_SLOT = {name: i for i, name in enumerate(SWAPS)}


def block(a, b):
    return ORDER.index((a, b))


def halves(v):
    high = v.astype(BF16)
    return high, (v - high.astype(F32)).astype(BF16)


def dot3(a, b):
    ah, al = halves(a)
    bh, bl = halves(b)
    return jnp.dot(
        jnp.concatenate([ah, ah, al], axis=1),
        jnp.concatenate([bh, bl, bh], axis=0),
        preferred_element_type=F32,
    )


def tdot(a, b):
    return lax.dot_general(a, b, (((0,), (0,)), ((), ())), preferred_element_type=F32)


def tdot3(a, b):
    ah, al = halves(a)
    bh, bl = halves(b)
    return tdot(jnp.concatenate([ah, ah, al], axis=0), jnp.concatenate([bh, bl, bh], axis=0))


def dot_full(a, b):
    return jnp.dot(a, b, precision=lax.Precision.HIGHEST, preferred_element_type=F32)


def thirds(v):
    high = v.astype(BF16)
    rest = v - high.astype(F32)
    middle = rest.astype(BF16)
    low = (rest - middle.astype(F32)).astype(BF16)
    return high, middle, low


def sweep(a_ref, column_ref, q_ref, log_ref, tasks):
    lane = lax.broadcasted_iota(jnp.int32, (STEP, R), 1)
    sub = lax.broadcasted_iota(jnp.int32, (STEP, R), 0)
    sub8 = lax.broadcasted_iota(jnp.int32, (8, R), 0)
    row_step = lax.broadcasted_iota(jnp.int32, (R, R), 0) // STEP
    column_step = lax.broadcasted_iota(jnp.int32, (R, R), 1) // STEP

    def pack(rows):
        groups = []
        for first in range(0, STEP, 8):
            packed = rows[first]
            for i in range(1, 8):
                packed = jnp.where(sub8 == i, rows[first + i], packed)
            groups.append(packed)
        return jnp.concatenate(groups, axis=0)

    def step(p, carry):
        for at, task in tasks.items():
            pl.when(p == at)(task)
        base = pl.multiple_of(p * STEP, STEP)
        panel = a_ref[pl.ds(base, STEP), :]
        turned = pltpu.roll(panel, lax.rem(R - base, R), axis=1)
        for j in range(STEP):
            high = (j // 8 + 1) * 8
            column_ref[pl.ds(j * STEP, high), :] = jnp.broadcast_to(turned[:high, j : j + 1], (high, R))
        q_ref[pl.ds(0, STEP), :] = jnp.where(
            lane // STEP == p, jnp.where(lane - base == sub, -1.0, 0.0), panel
        )
        rows, ratios, inverses = [], [], []
        for i in range(STEP):
            row = [column_ref[pl.ds(j * STEP + i, 8, stride=0), :] for j in range(i, STEP)]
            row.append(q_ref[pl.ds(i, 8, stride=0), :])
            row = jnp.stack(row)
            for m in range(i):
                row = row - ratios[m][i - m][None] * rows[m][i - m :]
            inverse = 1.0 / row[0]
            rows.append(row)
            inverses.append(inverse)
            ratios.append(row[: STEP - i] * inverse[None])
        v = pack([rows[i][STEP - i] for i in range(STEP)])
        w = v * pack(inverses)
        pivots = pack([rows[i][0] for i in range(STEP)])
        vh, vm, vl = thirds(v)
        wh, wm, wl = thirds(w)
        change = tdot(
            jnp.concatenate([vh, vh, vm, vh, vm, vl], axis=0),
            jnp.concatenate([wh, wm, wh, wl, wm, wh], axis=0),
        )
        a_ref[...] = jnp.where((row_step == p) | (column_step == p), 0.0, a_ref[...]) - change
        taken = jnp.log(pivots)
        log_ref[...] = log_ref[...] + taken[:8] + taken[8:]
        return carry

    lax.fori_loop(0, R // STEP, step, 0)


def kernel(
    d_hbm, u_hbm, b_hbm, ab_hbm, weights_ref, total_ref,
    dv, uv, bv, xv, ab, g, rd, rs, rta, rtb, ra, rb, ha, hb, qa, qb,
    pc, sx, rx, dx, dr, f, iv, tv, gt, zv, a_ref, column_ref, q_ref, log_ref,
    load_sem, out_sem, rs_send, rs_recv, d_send, d_recv, x_send, x_recv, g_send, g_recv,
):
    leaves = d_hbm.shape[0]
    size = d_hbm.shape[1]

    me = lax.axis_index("leaf")
    z = me // 32
    x = (me // 8) % 4
    half = x // 2
    x_in = x + half * (3 - 2 * x)
    seat = x_in * 8 + me % 8
    chip = seat // 2
    core = seat % 2
    piece = pl.multiple_of(seat * 8, 8)

    def device(other):
        xo = other // 8
        return z * 32 + (xo + half * (3 - 2 * xo)) * 8 + other % 8

    mate = me + 1 - 2 * core
    partner = (
        None,
        me + 8 * (3 - 2 * x),
        me + 32 * (1 - 2 * (z % 2)),
        me + 32 * (3 - 2 * (z % 4)),
        me + 32 * (7 - 2 * z),
    )

    def rows_of(leaf):
        return pl.ds(pl.multiple_of(leaf * size, size), size)

    def load_d(leaf):
        return pltpu.make_async_copy(d_hbm.at[leaf], dv.at[leaf], load_sem.at[0, leaf])

    def load_u(leaf, first, count, slot):
        at = (pl.ds(first, count), rows_of(leaf), slice(None))
        return pltpu.make_async_copy(u_hbm.at[at], uv.at[at], load_sem.at[slot, leaf])

    def load_b(leaf):
        return pltpu.make_async_copy(b_hbm.at[rows_of(leaf), :], bv.at[rows_of(leaf), :], load_sem.at[4, leaf])

    for leaf in range(leaves):
        load_d(leaf).start()
        load_u(leaf, 0, 2, 1).start()
    barrier = pltpu.get_barrier_semaphore()

    def greet(r, carry):
        pl.semaphore_signal(barrier, inc=1, device_id=(device((seat + r) % GROUP),), device_id_type=MESH)
        return carry

    lax.fori_loop(1, GROUP, greet, 0)
    for e in range(1, LEVELS):
        pl.semaphore_signal(barrier, inc=1, device_id=(partner[e],), device_id_type=MESH)

    for leaf in range(leaves):
        load_u(leaf, 2, 2, 2).start()
    for leaf in range(leaves):
        load_u(leaf, 4, 1, 3).start()
        load_b(leaf).start()

    def remote(source, target, send, recv, who):
        return pltpu.make_async_remote_copy(
            src_ref=source, dst_ref=target, send_sem=send, recv_sem=recv,
            device_id=(who,), device_id_type=MESH,
        )

    def columns_of(columns):
        top = min(columns[-1], LEVELS - 1)
        u = [uv[j] for j in range(top + 1)]
        have = [u[k] if k < LEVELS else bv[...] for k in columns]
        high, low = halves(jnp.concatenate(have, axis=1))
        got = []
        for leaf in range(leaves):
            at = slice(size * leaf, size * (leaf + 1))
            d_high, d_low = halves(dv[leaf])
            got.append(
                jnp.dot(
                    jnp.concatenate([d_high, d_high, d_low], axis=1),
                    jnp.concatenate([high[at], low[at], high[at]], axis=0),
                    preferred_element_type=F32,
                )
            )
        got = jnp.concatenate(got, axis=0)
        products = tdot3(jnp.concatenate(u, axis=1), got)
        for i, k in enumerate(columns):
            xv[k] = got[:, R * i : R * (i + 1)]
            for j in range(min(k, LEVELS - 1) + 1):
                g[block(j, k)] = products[R * j : R * (j + 1), R * i : R * (i + 1)].reshape(8, 2, 8, R)

    def scatter(first, count, target, slot):
        def one(r, carry):
            other = (seat + r) % GROUP
            remote(
                g.at[pl.ds(first, count), other // 2, other % 2], target.at[r - 1],
                rs_send.at[slot], rs_recv.at[slot], device(other),
            ).start()
            return carry

        lax.fori_loop(1, GROUP, one, 0, unroll=5)

    def scattered(first, count, target, slot):
        remote(target, target, rs_send.at[slot], rs_recv.at[slot], me).wait_recv()
        kept = g[pl.ds(first, count), chip, core]
        for r in range(GROUP - 1):
            kept = kept + target[r]
        pc[pl.ds(first, count)] = kept

    def to_mate(blocks, target, slot):
        first, last = blocks
        return remote(
            g.at[pl.ds(first, last - first), pl.ds(0, 8), 1 - core], target, rs_send.at[slot], rs_recv.at[slot], mate
        )

    def scatter_chips(blocks, from_mate, summed, target, slot):
        first, last = blocks
        to_mate(blocks, from_mate, slot - 1).wait_recv()

        def add(i, carry):
            summed[i] = g[i + first, :, core] + from_mate[i]
            return carry

        lax.fori_loop(0, last - first, add, 0)

        def one(r, carry):
            other = (chip + r) % 8
            remote(
                summed.at[pl.ds(0, last - first), other], target.at[r - 1],
                rs_send.at[slot], rs_recv.at[slot], device(other * 2 + core),
            ).start()
            return carry

        lax.fori_loop(1, 8, one, 0, unroll=True)

    def scattered_chips(blocks, summed, target, slot):
        first, last = blocks
        remote(target, target, rs_send.at[slot], rs_recv.at[slot], me).wait_recv()
        kept = summed[:, chip]
        for r in range(7):
            kept = kept + target[r]
        pc[pl.ds(first, last - first)] = kept

    def gather(name):
        first, last = GATHERS[name]
        slot = GATHER_SLOT[name]
        f[pl.ds(first, last - first), pl.ds(piece, 8), :] = pc[pl.ds(first, last - first)]

        def one(r, carry):
            other = (seat + r) % GROUP
            remote(
                pc.at[pl.ds(first, last - first)],
                f.at[pl.ds(first, last - first), pl.ds(piece, 8), :],
                g_send.at[slot], g_recv.at[slot], device(other),
            ).start()
            return carry

        lax.fori_loop(1, GROUP, one, 0, unroll=5)

    def gathered(name):
        first, last = GATHERS[name]
        slot = GATHER_SLOT[name]
        ref = f.at[pl.ds(first, last - first), pl.ds(0, 120), :]
        return remote(ref, ref, g_send.at[slot], g_recv.at[slot], me)

    def diagonal(e):
        return remote(dx.at[e - 1], dr.at[e - 1], d_send.at[e - 1], d_recv.at[e - 1], partner[e])

    def swap(name):
        first, last = SWAPS[name]
        e = int(name[1])
        slot = SWAP_SLOT[name]
        at = pl.ds(first, last - first)
        return remote(sx.at[e - 1, at], rx.at[e - 1, at], x_send.at[slot], x_recv.at[slot], partner[e])

    def whole(a, b):
        return f[block(a, b)]

    def turn(level, k):
        gt[level, k] = whole(level, k).T

    def critical(level):
        e = level + 1
        ratio = dot_full(iv[level], whole(level, e))
        tv[level, e] = ratio
        dx[e - 1, pl.ds(0, R), :] = whole(e, e) - dot_full(gt[level, e], ratio)
        dx[e - 1, pl.ds(R, 8), :] = log_ref[...]
        diagonal(e).start()

    def lower(level, columns, name):
        e = level + 1
        first, last = SWAPS[name]
        fresh = [k for k in columns if k != e]
        ratio = dot3(iv[level], jnp.concatenate([whole(level, k) for k in fresh], axis=1))
        for i, k in enumerate(fresh):
            tv[level, k] = ratio[:, R * i : R * (i + 1)]
            if k < LEVELS:
                turn(level, k)
        ends = [r for r in range(e, LEVELS) if r <= columns[-1]]
        left = jnp.concatenate([gt[level, r, pl.ds(piece, 8), :] for r in ends], axis=0)
        down = dot3(left, ratio)
        for at in range(first, last):
            r, k = ORDER[at]
            i = fresh.index(k)
            sx[e - 1, at] = pc[at] - down[8 * (r - e) : 8 * (r - e) + 8, R * i : R * (i + 1)]
        swap(name).start()

    def merge(name, *sets):
        first, last = SWAPS[name]
        e = int(name[1])
        swap(name).wait_recv()
        at = pl.ds(first, last - first)
        pc[at] = sx[e - 1, at] + rx[e - 1, at]
        for each in sets:
            gather(each)

    def enter(e):
        diagonal(e).wait_recv()
        a_ref[...] = dx[e - 1, pl.ds(0, R), :] + dr[e - 1, pl.ds(0, R), :] + eye
        log_ref[...] = dx[e - 1, pl.ds(R, 8), :] + dr[e - 1, pl.ds(R, 8), :]

    def invert(level, tasks):
        sweep(a_ref, column_ref, q_ref, log_ref, tasks)
        iv[level] = -a_ref[...]

    eye = (
        lax.broadcasted_iota(jnp.int32, (R, R), 0) == lax.broadcasted_iota(jnp.int32, (R, R), 1)
    ).astype(F32)

    for leaf in range(leaves):
        load_d(leaf).wait()
        load_u(leaf, 0, 2, 1).wait()
    columns_of((0, 1))
    pl.semaphore_wait(barrier, GROUP - 1 + LEVELS - 1)
    scatter(0, 1, rd, 0)
    scatter(1, 2, rs, 1)
    for leaf in range(leaves):
        load_u(leaf, 2, 2, 2).wait()
    columns_of((2, 3))
    scatter(3, 2, rta, 2)
    to_mate(A, ra, 4).start()
    scattered(0, 1, rd, 0)
    gather("d0")
    for leaf in range(leaves):
        load_u(leaf, 4, 1, 3).wait()
        load_b(leaf).wait()
    columns_of((4, 5))
    scatter(10, 2, rtb, 3)
    to_mate(B, rb, 6).start()
    scattered(1, 2, rs, 1)
    gather("c0")
    scatter_chips(A, ra, ha, qa, 5)
    gathered("d0").wait_recv()
    a_ref[...] = whole(0, 0) + eye
    log_ref[...] = jnp.zeros((8, R), F32)

    def task_0a():
        scattered(3, 2, rta, 2)
        gather("a0")

    def task_0b():
        scatter_chips(B, rb, hb, qb, 7)

    def task_0c():
        scattered(10, 2, rtb, 3)
        gather("b0")

    invert(0, {1: task_0a, 3: task_0b, 5: task_0c})
    gathered("c0").wait_recv()
    turn(0, 1)
    critical(0)
    scattered_chips(A, ha, qa, 5)
    gathered("a0").wait_recv()
    lower(0, (2, 3), "a1")
    scattered_chips(B, hb, qb, 7)
    gathered("b0").wait_recv()
    lower(0, (4, 5), "b1")

    enter(1)
    merge("a1", "a1", "e1")

    def task_1():
        merge("b1", "b1")

    invert(1, {3: task_1})
    gathered("a1").wait_recv()
    turn(1, 2)
    critical(1)
    gathered("e1").wait_recv()
    lower(1, (2, 3), "a2")
    gathered("b1").wait_recv()
    lower(1, (4, 5), "b2")

    enter(2)
    merge("a2", "a2")

    def task_2():
        merge("b2", "b2")

    invert(2, {3: task_2})
    gathered("a2").wait_recv()
    turn(2, 3)
    critical(2)
    gathered("b2").wait_recv()
    lower(2, (4, 5), "b3")

    enter(3)
    merge("b3", "b3", "e3")
    invert(3, {})
    gathered("b3").wait_recv()
    turn(3, 4)
    critical(3)
    gathered("e3").wait_recv()
    lower(3, (4, 5), "b4")

    for level in range(LEVELS - 2, -1, -1):
        pair = jnp.concatenate([tv[level, 4], tv[level, 5]], axis=1)
        if level < LEVELS - 2:
            between = jnp.concatenate([tv[level, k] for k in range(level + 1, LEVELS - 1)], axis=1)
            pair = pair - dot3(between, zv[pl.ds(R * (level + 1), R * (LEVELS - 2 - level)), :])
        zv[pl.ds(R * level, R), :] = pair
    z_high, z_low = halves(zv[...])
    z_stack = jnp.concatenate([z_high, z_low, z_high], axis=0)

    high, low = halves(jnp.concatenate([xv[k] for k in range(LEVELS - 1)], axis=1))
    change = jnp.dot(jnp.concatenate([high, high, low], axis=1), z_stack, preferred_element_type=F32)
    ab[...] = jnp.concatenate([xv[k] for k in (4, 5)], axis=1) - change
    leave = pltpu.make_async_copy(ab, ab_hbm, out_sem)
    leave.start()

    merge("b4", "b4")
    enter(4)
    invert(4, {})
    gathered("b4").wait_recv()
    weights_ref[...] = dot_full(iv[4], whole(4, 5))
    total_ref[0, 0] = jnp.sum(log_ref[...]) / (R * R * (2**LEVELS - 1))

    for target, slot in ((rd, 0), (rs, 1), (rta, 2), (rtb, 3), (qa, 5), (qb, 7)):
        remote(target, target, rs_send.at[slot], rs_recv.at[slot], me).wait_send()
    to_mate(A, ra, 4).wait_send()
    to_mate(B, rb, 6).wait_send()
    for name in GATHERS:
        gathered(name).wait_send()
    for name in SWAPS:
        swap(name).wait_send()
    for e in range(1, LEVELS):
        diagonal(e).wait_send()

    leave.wait()


def finish(columns_ref, weights_ref, total_ref, o_ref, log_ref):
    o_ref[...] = columns_ref[:, R:] - dot3(columns_ref[:, :R], weights_ref[...])

    @pl.when(pl.program_id(0) == 0)
    def _():
        log_ref[0, 0] = total_ref[0, 0]


def body(leaf_inverse, node_bases, right_sides):
    leaves, size = leaf_inverse.shape[:2]
    rows = right_sides.shape[0]
    bases = jnp.transpose(node_bases, (1, 0, 2))
    any_spec = pl.BlockSpec(memory_space=pl.ANY)
    na, nb = A[1] - A[0], B[1] - B[0]
    shapes = [
        (leaves, size, size), (LEVELS, rows, R), (rows, R), (LEVEL_COLUMNS, rows, R), (rows, 2 * R),
        (COUNT, 8, 2, 8, R), (GROUP - 1, 1, 8, R), (GROUP - 1, 2, 8, R), (GROUP - 1, 2, 8, R), (GROUP - 1, 2, 8, R),
        (na, 8, 8, R), (nb, 8, 8, R), (na, 8, 8, R), (nb, 8, 8, R), (7, na, 8, R), (7, nb, 8, R),
        (COUNT, 8, R), (LEVELS - 1, COUNT, 8, R), (LEVELS - 1, COUNT, 8, R),
        (LEVELS - 1, R + 8, R), (LEVELS - 1, R + 8, R), (COUNT, R, R), (LEVELS, R, R),
        (LEVELS - 1, LEVEL_COLUMNS, R, R), (LEVELS - 1, LEVELS, R, R), ((LEVELS - 1) * R, 2 * R), (R, R),
        (STEP * STEP + 8, R), (STEP + 8, R), (8, R),
    ]
    dma = pltpu.SemaphoreType.DMA
    scratch = [pltpu.VMEM(shape, F32) for shape in shapes]
    scratch += [
        dma((5, leaves)), dma(()), dma((8,)), dma((8,)), dma((LEVELS - 1,)), dma((LEVELS - 1,)),
        dma((len(SWAPS),)), dma((len(SWAPS),)), dma((len(GATHERS),)), dma((len(GATHERS),)),
    ]
    smem = pl.BlockSpec(memory_space=pltpu.SMEM)
    columns, weights, total = pl.pallas_call(
        kernel,
        out_shape=(
            jax.ShapeDtypeStruct((rows, 2 * R), F32),
            jax.ShapeDtypeStruct((R, R), F32),
            jax.ShapeDtypeStruct((1, 1), F32),
        ),
        in_specs=[any_spec] * 3,
        out_specs=(any_spec, pl.BlockSpec(memory_space=pltpu.VMEM), smem),
        scratch_shapes=scratch,
        compiler_params=pltpu.CompilerParams(
            collective_id=0, has_side_effects=True, vmem_limit_bytes=60 * 2**20
        ),
    )(leaf_inverse, bases, right_sides)
    part = rows // 2
    solution, log_total = pl.pallas_call(
        finish,
        grid=(2,),
        out_shape=(
            jax.ShapeDtypeStruct((rows, R), F32),
            jax.ShapeDtypeStruct((1, 1), F32),
        ),
        in_specs=[
            pl.BlockSpec((part, 2 * R), lambda i: (i, 0)),
            pl.BlockSpec((R, R), lambda i: (0, 0)),
            smem,
        ],
        out_specs=(pl.BlockSpec((part, R), lambda i: (i, 0)), smem),
    )(columns, weights, total)
    return solution, log_total.reshape(())


def solution(mesh):
    return jax.shard_map(
        body,
        mesh=mesh,
        in_specs=(P("leaf", None, None), P("leaf", None, None), P("leaf", None)),
        out_specs=(P("leaf", None), P()),
        check_vma=False,
    )
```

```python
import functools

import jax
import jax.numpy as jnp
from jax import lax
from jax.experimental import pallas as pl
from jax.experimental.pallas import tpu as pltpu
from jax.sharding import PartitionSpec as P

F32 = jnp.float32
BF16 = jnp.bfloat16
MESH = pl.DeviceIdType.MESH
R = 128
LEVELS = 5
LEVEL_COLUMNS = LEVELS + 1
GROUP = 16
STEP = 16

ORDER = (
    (0, 0), (0, 1), (1, 1),
    (0, 2), (0, 3), (1, 2), (2, 2), (1, 3), (2, 3), (3, 3),
    (0, 4), (0, 5), (1, 4), (1, 5), (2, 4), (2, 5), (3, 4), (4, 4), (3, 5), (4, 5),
)
COUNT = len(ORDER)
A, B = (5, 10), (12, 20)
GATHERS = {
    "d0": (0, 1), "c0": (1, 3), "a0": (3, 5), "b0": (10, 12), "a1": (5, 7), "e1": (7, 8), "b1": (12, 14),
    "a2": (8, 10), "b2": (14, 16), "b3": (16, 18), "e3": (18, 19), "b4": (19, 20),
}
SWAPS = {"a1": (5, 10), "b1": (12, 20), "a2": (8, 10), "b2": (14, 20), "b3": (16, 20), "b4": (19, 20)}
GATHER_SLOT = {name: i for i, name in enumerate(GATHERS)}
SWAP_SLOT = {name: i for i, name in enumerate(SWAPS)}


def block(a, b):
    return ORDER.index((a, b))


def halves(v):
    high = v.astype(BF16)
    return high, (v - high.astype(F32)).astype(BF16)


def dot3(a, b):
    ah, al = halves(a)
    bh, bl = halves(b)
    return jnp.dot(
        jnp.concatenate([ah, ah, al], axis=1),
        jnp.concatenate([bh, bl, bh], axis=0),
        preferred_element_type=F32,
    )


def tdot(a, b):
    return lax.dot_general(a, b, (((0,), (0,)), ((), ())), preferred_element_type=F32)


def tdot3(a, b):
    ah, al = halves(a)
    bh, bl = halves(b)
    return tdot(jnp.concatenate([ah, ah, al], axis=0), jnp.concatenate([bh, bl, bh], axis=0))


def dot_full(a, b):
    return jnp.dot(a, b, precision=lax.Precision.HIGHEST, preferred_element_type=F32)


def thirds(v):
    high = v.astype(BF16)
    rest = v - high.astype(F32)
    middle = rest.astype(BF16)
    low = (rest - middle.astype(F32)).astype(BF16)
    return high, middle, low


def sweep(a_ref, column_ref, q_ref, log_ref, tasks):
    lane = lax.broadcasted_iota(jnp.int32, (STEP, R), 1)
    sub = lax.broadcasted_iota(jnp.int32, (STEP, R), 0)
    sub8 = lax.broadcasted_iota(jnp.int32, (8, R), 0)
    row_step = lax.broadcasted_iota(jnp.int32, (R, R), 0) // STEP
    column_step = lax.broadcasted_iota(jnp.int32, (R, R), 1) // STEP

    def pack(rows):
        groups = []
        for first in range(0, STEP, 8):
            packed = rows[first]
            for i in range(1, 8):
                packed = jnp.where(sub8 == i, rows[first + i], packed)
            groups.append(packed)
        return jnp.concatenate(groups, axis=0)

    def step(p, carry):
        for at, task in tasks.items():
            pl.when(p == at)(task)
        base = pl.multiple_of(p * STEP, STEP)
        panel = a_ref[pl.ds(base, STEP), :]
        turned = pltpu.roll(panel, lax.rem(R - base, R), axis=1)
        for j in range(STEP):
            high = (j // 8 + 1) * 8
            column_ref[pl.ds(j * STEP, high), :] = jnp.broadcast_to(turned[:high, j : j + 1], (high, R))
        q_ref[pl.ds(0, STEP), :] = jnp.where(
            lane // STEP == p, jnp.where(lane - base == sub, -1.0, 0.0), panel
        )
        rows, ratios, inverses = [], [], []
        for i in range(STEP):
            row = [column_ref[pl.ds(j * STEP + i, 8, stride=0), :] for j in range(i, STEP)]
            row.append(q_ref[pl.ds(i, 8, stride=0), :])
            row = jnp.stack(row)
            for m in range(i):
                row = row - ratios[m][i - m][None] * rows[m][i - m :]
            inverse = 1.0 / row[0]
            rows.append(row)
            inverses.append(inverse)
            ratios.append(row[: STEP - i] * inverse[None])
        v = pack([rows[i][STEP - i] for i in range(STEP)])
        w = v * pack(inverses)
        pivots = pack([rows[i][0] for i in range(STEP)])
        vh, vm, vl = thirds(v)
        wh, wm, wl = thirds(w)
        change = tdot(
            jnp.concatenate([vh, vh, vm, vh, vm, vl], axis=0),
            jnp.concatenate([wh, wm, wh, wl, wm, wh], axis=0),
        )
        a_ref[...] = jnp.where((row_step == p) | (column_step == p), 0.0, a_ref[...]) - change
        taken = jnp.log(pivots)
        log_ref[...] = log_ref[...] + taken[:8] + taken[8:]
        return carry

    lax.fori_loop(0, R // STEP, step, 0)


def kernel(
    d_hbm, u_hbm, b_hbm, ab_hbm, weights_ref, total_ref,
    dv, uv, bv, xv, ab, g, rd, rs, rta, rtb, ra, rb, ha, hb, qa, qb,
    pc, sx, rx, dx, dr, f, iv, tv, gt, zv, a_ref, column_ref, q_ref, log_ref,
    load_sem, out_sem, rs_send, rs_recv, d_send, d_recv, x_send, x_recv, g_send, g_recv,
):
    leaves = d_hbm.shape[0]
    size = d_hbm.shape[1]

    me = lax.axis_index("leaf")
    z = me // 32
    x = (me // 8) % 4
    half = x // 2
    x_in = x + half * (3 - 2 * x)
    seat = x_in * 8 + me % 8
    chip = seat // 2
    core = seat % 2
    piece = pl.multiple_of(seat * 8, 8)

    def device(other):
        xo = other // 8
        return z * 32 + (xo + half * (3 - 2 * xo)) * 8 + other % 8

    mate = me + 1 - 2 * core
    partner = (
        None,
        me + 8 * (3 - 2 * x),
        me + 32 * (1 - 2 * (z % 2)),
        me + 32 * (3 - 2 * (z % 4)),
        me + 32 * (7 - 2 * z),
    )

    def rows_of(leaf):
        return pl.ds(pl.multiple_of(leaf * size, size), size)

    def load_d(leaf):
        return pltpu.make_async_copy(d_hbm.at[leaf], dv.at[leaf], load_sem.at[0, leaf])

    def load_u(leaf, first, count, slot):
        at = (pl.ds(first, count), rows_of(leaf), slice(None))
        return pltpu.make_async_copy(u_hbm.at[at], uv.at[at], load_sem.at[slot, leaf])

    def load_b(leaf):
        return pltpu.make_async_copy(b_hbm.at[rows_of(leaf), :], bv.at[rows_of(leaf), :], load_sem.at[4, leaf])

    for leaf in range(leaves):
        load_d(leaf).start()
        load_u(leaf, 0, 2, 1).start()
    barrier = pltpu.get_barrier_semaphore()

    def greet(r, carry):
        pl.semaphore_signal(barrier, inc=1, device_id=(device((seat + r) % GROUP),), device_id_type=MESH)
        return carry

    lax.fori_loop(1, GROUP, greet, 0)
    for e in range(1, LEVELS):
        pl.semaphore_signal(barrier, inc=1, device_id=(partner[e],), device_id_type=MESH)

    for leaf in range(leaves):
        load_u(leaf, 2, 2, 2).start()
    for leaf in range(leaves):
        load_u(leaf, 4, 1, 3).start()
        load_b(leaf).start()

    def remote(source, target, send, recv, who):
        return pltpu.make_async_remote_copy(
            src_ref=source, dst_ref=target, send_sem=send, recv_sem=recv,
            device_id=(who,), device_id_type=MESH,
        )

    def columns_of(columns):
        top = min(columns[-1], LEVELS - 1)
        u = [uv[j] for j in range(top + 1)]
        have = [u[k] if k < LEVELS else bv[...] for k in columns]
        high, low = halves(jnp.concatenate(have, axis=1))
        got = []
        for leaf in range(leaves):
            at = slice(size * leaf, size * (leaf + 1))
            d_high, d_low = halves(dv[leaf])
            got.append(
                jnp.dot(
                    jnp.concatenate([d_high, d_high, d_low], axis=1),
                    jnp.concatenate([high[at], low[at], high[at]], axis=0),
                    preferred_element_type=F32,
                )
            )
        got = jnp.concatenate(got, axis=0)
        products = tdot3(jnp.concatenate(u, axis=1), got)
        for i, k in enumerate(columns):
            xv[k] = got[:, R * i : R * (i + 1)]
            for j in range(min(k, LEVELS - 1) + 1):
                g[block(j, k)] = products[R * j : R * (j + 1), R * i : R * (i + 1)].reshape(8, 2, 8, R)

    def scatter(first, count, target, slot):
        def one(r, carry):
            other = (seat + r) % GROUP
            remote(
                g.at[pl.ds(first, count), other // 2, other % 2], target.at[r - 1],
                rs_send.at[slot], rs_recv.at[slot], device(other),
            ).start()
            return carry

        lax.fori_loop(1, GROUP, one, 0, unroll=5)

    def scattered(first, count, target, slot):
        remote(target, target, rs_send.at[slot], rs_recv.at[slot], me).wait_recv()
        kept = g[pl.ds(first, count), chip, core]
        for r in range(GROUP - 1):
            kept = kept + target[r]
        pc[pl.ds(first, count)] = kept

    def to_mate(blocks, target, slot):
        first, last = blocks
        return remote(
            g.at[pl.ds(first, last - first), pl.ds(0, 8), 1 - core], target, rs_send.at[slot], rs_recv.at[slot], mate
        )

    def scatter_chips(blocks, from_mate, summed, target, slot):
        first, last = blocks
        to_mate(blocks, from_mate, slot - 1).wait_recv()

        def add(i, carry):
            summed[i] = g[i + first, :, core] + from_mate[i]
            return carry

        lax.fori_loop(0, last - first, add, 0)

        def one(r, carry):
            other = (chip + r) % 8
            remote(
                summed.at[pl.ds(0, last - first), other], target.at[r - 1],
                rs_send.at[slot], rs_recv.at[slot], device(other * 2 + core),
            ).start()
            return carry

        lax.fori_loop(1, 8, one, 0, unroll=True)

    def scattered_chips(blocks, summed, target, slot):
        first, last = blocks
        remote(target, target, rs_send.at[slot], rs_recv.at[slot], me).wait_recv()
        kept = summed[:, chip]
        for r in range(7):
            kept = kept + target[r]
        pc[pl.ds(first, last - first)] = kept

    def gather(name):
        first, last = GATHERS[name]
        slot = GATHER_SLOT[name]
        f[pl.ds(first, last - first), pl.ds(piece, 8), :] = pc[pl.ds(first, last - first)]

        def one(r, carry):
            other = (seat + r) % GROUP
            remote(
                pc.at[pl.ds(first, last - first)],
                f.at[pl.ds(first, last - first), pl.ds(piece, 8), :],
                g_send.at[slot], g_recv.at[slot], device(other),
            ).start()
            return carry

        lax.fori_loop(1, GROUP, one, 0, unroll=5)

    def gathered(name):
        first, last = GATHERS[name]
        slot = GATHER_SLOT[name]
        ref = f.at[pl.ds(first, last - first), pl.ds(0, 120), :]
        return remote(ref, ref, g_send.at[slot], g_recv.at[slot], me)

    def diagonal(e):
        return remote(dx.at[e - 1], dr.at[e - 1], d_send.at[e - 1], d_recv.at[e - 1], partner[e])

    def swap(name):
        first, last = SWAPS[name]
        e = int(name[1])
        slot = SWAP_SLOT[name]
        at = pl.ds(first, last - first)
        return remote(sx.at[e - 1, at], rx.at[e - 1, at], x_send.at[slot], x_recv.at[slot], partner[e])

    def whole(a, b):
        return f[block(a, b)]

    def turn(level, k):
        gt[level, k] = whole(level, k).T

    def critical(level):
        e = level + 1
        ratio = dot_full(iv[level], whole(level, e))
        tv[level, e] = ratio
        dx[e - 1, pl.ds(0, R), :] = whole(e, e) - dot_full(gt[level, e], ratio)
        dx[e - 1, pl.ds(R, 8), :] = log_ref[...]
        diagonal(e).start()

    def lower(level, columns, name):
        e = level + 1
        first, last = SWAPS[name]
        fresh = [k for k in columns if k != e]
        ratio = dot3(iv[level], jnp.concatenate([whole(level, k) for k in fresh], axis=1))
        for i, k in enumerate(fresh):
            tv[level, k] = ratio[:, R * i : R * (i + 1)]
            if k < LEVELS:
                turn(level, k)
        ends = [r for r in range(e, LEVELS) if r <= columns[-1]]
        left = jnp.concatenate([gt[level, r, pl.ds(piece, 8), :] for r in ends], axis=0)
        down = dot3(left, ratio)
        for at in range(first, last):
            r, k = ORDER[at]
            i = fresh.index(k)
            sx[e - 1, at] = pc[at] - down[8 * (r - e) : 8 * (r - e) + 8, R * i : R * (i + 1)]
        swap(name).start()

    def merge(name, *sets):
        first, last = SWAPS[name]
        e = int(name[1])
        swap(name).wait_recv()
        at = pl.ds(first, last - first)
        pc[at] = sx[e - 1, at] + rx[e - 1, at]
        for each in sets:
            gather(each)

    def enter(e):
        diagonal(e).wait_recv()
        a_ref[...] = dx[e - 1, pl.ds(0, R), :] + dr[e - 1, pl.ds(0, R), :] + eye
        log_ref[...] = dx[e - 1, pl.ds(R, 8), :] + dr[e - 1, pl.ds(R, 8), :]

    def invert(level, tasks):
        sweep(a_ref, column_ref, q_ref, log_ref, tasks)
        iv[level] = -a_ref[...]

    eye = (
        lax.broadcasted_iota(jnp.int32, (R, R), 0) == lax.broadcasted_iota(jnp.int32, (R, R), 1)
    ).astype(F32)

    for leaf in range(leaves):
        load_d(leaf).wait()
        load_u(leaf, 0, 2, 1).wait()
    columns_of((0, 1))
    pl.semaphore_wait(barrier, GROUP - 1 + LEVELS - 1)
    scatter(0, 1, rd, 0)
    scatter(1, 2, rs, 1)
    for leaf in range(leaves):
        load_u(leaf, 2, 2, 2).wait()
    columns_of((2, 3))
    scatter(3, 2, rta, 2)
    to_mate(A, ra, 4).start()
    scattered(0, 1, rd, 0)
    gather("d0")
    for leaf in range(leaves):
        load_u(leaf, 4, 1, 3).wait()
        load_b(leaf).wait()
    columns_of((4, 5))
    scatter(10, 2, rtb, 3)
    to_mate(B, rb, 6).start()
    scattered(1, 2, rs, 1)
    gather("c0")
    scatter_chips(A, ra, ha, qa, 5)
    gathered("d0").wait_recv()
    a_ref[...] = whole(0, 0) + eye
    log_ref[...] = jnp.zeros((8, R), F32)

    def task_0a():
        scattered(3, 2, rta, 2)
        gather("a0")

    def task_0b():
        scatter_chips(B, rb, hb, qb, 7)

    def task_0c():
        scattered(10, 2, rtb, 3)
        gather("b0")

    invert(0, {1: task_0a, 2: task_0b, 4: task_0c})
    gathered("c0").wait_recv()
    turn(0, 1)
    critical(0)
    scattered_chips(A, ha, qa, 5)
    gathered("a0").wait_recv()
    lower(0, (2, 3), "a1")
    scattered_chips(B, hb, qb, 7)
    gathered("b0").wait_recv()
    lower(0, (4, 5), "b1")

    enter(1)
    merge("a1", "a1", "e1")

    def task_1():
        merge("b1", "b1")

    invert(1, {3: task_1})
    gathered("a1").wait_recv()
    turn(1, 2)
    critical(1)
    gathered("e1").wait_recv()
    lower(1, (2, 3), "a2")
    gathered("b1").wait_recv()
    lower(1, (4, 5), "b2")

    enter(2)
    merge("a2", "a2")

    def task_2():
        merge("b2", "b2")

    invert(2, {3: task_2})
    gathered("a2").wait_recv()
    turn(2, 3)
    critical(2)
    gathered("b2").wait_recv()
    lower(2, (4, 5), "b3")

    enter(3)
    merge("b3", "b3", "e3")
    invert(3, {})
    gathered("b3").wait_recv()
    turn(3, 4)
    critical(3)
    gathered("e3").wait_recv()
    lower(3, (4, 5), "b4")

    for level in range(LEVELS - 2, -1, -1):
        pair = jnp.concatenate([tv[level, 4], tv[level, 5]], axis=1)
        if level < LEVELS - 2:
            between = jnp.concatenate([tv[level, k] for k in range(level + 1, LEVELS - 1)], axis=1)
            pair = pair - dot3(between, zv[pl.ds(R * (level + 1), R * (LEVELS - 2 - level)), :])
        zv[pl.ds(R * level, R), :] = pair
    z_high, z_low = halves(zv[...])
    z_stack = jnp.concatenate([z_high, z_low, z_high], axis=0)

    high, low = halves(jnp.concatenate([xv[k] for k in range(LEVELS - 1)], axis=1))
    change = jnp.dot(jnp.concatenate([high, high, low], axis=1), z_stack, preferred_element_type=F32)
    ab[...] = jnp.concatenate([xv[k] for k in (4, 5)], axis=1) - change
    leave = pltpu.make_async_copy(ab, ab_hbm, out_sem)
    leave.start()

    merge("b4", "b4")
    enter(4)
    invert(4, {})
    gathered("b4").wait_recv()
    weights_ref[...] = dot_full(iv[4], whole(4, 5))
    total_ref[0, 0] = jnp.sum(log_ref[...]) / (R * R * (2**LEVELS - 1))

    for target, slot in ((rd, 0), (rs, 1), (rta, 2), (rtb, 3), (qa, 5), (qb, 7)):
        remote(target, target, rs_send.at[slot], rs_recv.at[slot], me).wait_send()
    to_mate(A, ra, 4).wait_send()
    to_mate(B, rb, 6).wait_send()
    for name in GATHERS:
        gathered(name).wait_send()
    for name in SWAPS:
        swap(name).wait_send()
    for e in range(1, LEVELS):
        diagonal(e).wait_send()

    leave.wait()


def finish(columns_ref, weights_ref, total_ref, o_ref, log_ref):
    o_ref[...] = columns_ref[:, R:] - dot3(columns_ref[:, :R], weights_ref[...])

    @pl.when(pl.program_id(0) == 0)
    def _():
        log_ref[0, 0] = total_ref[0, 0]


def body(leaf_inverse, node_bases, right_sides):
    leaves, size = leaf_inverse.shape[:2]
    rows = right_sides.shape[0]
    bases = jnp.transpose(node_bases, (1, 0, 2))
    any_spec = pl.BlockSpec(memory_space=pl.ANY)
    na, nb = A[1] - A[0], B[1] - B[0]
    shapes = [
        (leaves, size, size), (LEVELS, rows, R), (rows, R), (LEVEL_COLUMNS, rows, R), (rows, 2 * R),
        (COUNT, 8, 2, 8, R), (GROUP - 1, 1, 8, R), (GROUP - 1, 2, 8, R), (GROUP - 1, 2, 8, R), (GROUP - 1, 2, 8, R),
        (na, 8, 8, R), (nb, 8, 8, R), (na, 8, 8, R), (nb, 8, 8, R), (7, na, 8, R), (7, nb, 8, R),
        (COUNT, 8, R), (LEVELS - 1, COUNT, 8, R), (LEVELS - 1, COUNT, 8, R),
        (LEVELS - 1, R + 8, R), (LEVELS - 1, R + 8, R), (COUNT, R, R), (LEVELS, R, R),
        (LEVELS - 1, LEVEL_COLUMNS, R, R), (LEVELS - 1, LEVELS, R, R), ((LEVELS - 1) * R, 2 * R), (R, R),
        (STEP * STEP + 8, R), (STEP + 8, R), (8, R),
    ]
    dma = pltpu.SemaphoreType.DMA
    scratch = [pltpu.VMEM(shape, F32) for shape in shapes]
    scratch += [
        dma((5, leaves)), dma(()), dma((8,)), dma((8,)), dma((LEVELS - 1,)), dma((LEVELS - 1,)),
        dma((len(SWAPS),)), dma((len(SWAPS),)), dma((len(GATHERS),)), dma((len(GATHERS),)),
    ]
    smem = pl.BlockSpec(memory_space=pltpu.SMEM)
    columns, weights, total = pl.pallas_call(
        kernel,
        out_shape=(
            jax.ShapeDtypeStruct((rows, 2 * R), F32),
            jax.ShapeDtypeStruct((R, R), F32),
            jax.ShapeDtypeStruct((1, 1), F32),
        ),
        in_specs=[any_spec] * 3,
        out_specs=(any_spec, pl.BlockSpec(memory_space=pltpu.VMEM), smem),
        scratch_shapes=scratch,
        compiler_params=pltpu.CompilerParams(
            collective_id=0, has_side_effects=True, vmem_limit_bytes=60 * 2**20
        ),
    )(leaf_inverse, bases, right_sides)
    part = rows // 2
    solution, log_total = pl.pallas_call(
        finish,
        grid=(2,),
        out_shape=(
            jax.ShapeDtypeStruct((rows, R), F32),
            jax.ShapeDtypeStruct((1, 1), F32),
        ),
        in_specs=[
            pl.BlockSpec((part, 2 * R), lambda i: (i, 0)),
            pl.BlockSpec((R, R), lambda i: (0, 0)),
            smem,
        ],
        out_specs=(pl.BlockSpec((part, R), lambda i: (i, 0)), smem),
    )(columns, weights, total)
    return solution, log_total.reshape(())


def solution(mesh):
    return jax.shard_map(
        body,
        mesh=mesh,
        in_specs=(P("leaf", None, None), P("leaf", None, None), P("leaf", None)),
        out_specs=(P("leaf", None), P()),
        check_vma=False,
    )
```
